32 devices in a mesh: context: 8 (over z, x), tensor: 4 (over y, core).
Axes of the slice: x: 2, y: 2, z: 4, core: 2. Of those that a mesh axis runs over, the one named last changes fastest.
Arguments:
- length: int32 [1], replicated, may hold values from 512 to 1024
- mamba_in: bfloat16 [1024, 8192], P('context', 'tensor'), may hold values from -6 to 6
- gate_in: bfloat16 [1024, 8192], P('context', 'tensor'), may hold values from -6 to 6
- step_raw: bfloat16 [1024, 8192], P('context', 'tensor'), may hold values from -3 to 3
- conv_weight: float32 [4, 8192], P(None, 'tensor'), may hold values from -3 to 3
- conv_bias: float32 [8192], P('tensor'), may hold values from -3 to 3
- step_bias: float32 [8192], P('tensor'), may hold values from -1 to 1
- decay_rates: float32 [16, 8192], P(None, 'tensor'), may hold values from 4.8828126e-05 to 0.04
- skip_gain: float32 [8192], P('tensor'), may hold values from 0.5 to 1.5
- state_proj: bfloat16 [8192, 32], P('tensor'), may hold values from -0.015625 to 0.015625
- query_input_rows: bfloat16 [1024, 4096], P('context', 'tensor'), may hold values from -113.60155108391487 to 113.60155108391487
- key_input_rows: bfloat16 [1024, 512], P('context', 'tensor'), may hold values from -4 to 4
- value_input_rows: bfloat16 [1024, 512], P('context', 'tensor'), may hold values from -6 to 6
Outputs:
- mamba_out: bfloat16 [1024, 8192], P('context', 'tensor')
- attn_out: bfloat16 [1024, 4096], P('context', 'tensor')
The draws below stay inside these ranges and needn't reach their ends.
All inputs are finite; a program needn't handle non-finite values.
Results may differ from the reference program's by a relative error of at most 0.0085.
Values may be sent and summed in bfloat16 or wider, within the bound.
A program may use at most 128 MiB of HBM per device.

```python
import math
import jax
import jax.numpy as jnp
from jax import lax

DI = 8192
NS = 16
KW = 4
HEAD_WIDTH = 128
QUERY_HEADS = 32
KEY_VALUE_HEADS = 4
PROMPT_TOKENS = 1024


def key_head_table(key):
    base_offset = jax.random.normal(jax.random.fold_in(key, 11), (PROMPT_TOKENS, KEY_VALUE_HEADS * HEAD_WIDTH), jnp.float32)
    return jnp.clip(base_offset, -4.0, 4.0)


def draw_key_input_rows(key, part):
    return key_head_table(key).astype(jnp.bfloat16)


def draw_query_input_rows(key, part):
    base_offset = jax.random.normal(jax.random.fold_in(key, 23), (PROMPT_TOKENS, QUERY_HEADS * HEAD_WIDTH), jnp.float32)
    base_offset = jnp.clip(base_offset, -4.0, 4.0)
    return base_offset.astype(jnp.bfloat16)


def levels(stream_key, shape, split, least, largest):
    factor_of, own = 1.0, jax.random.fold_in(stream_key, 6)
    for dim, shards_of in split:
        draws = jnp.exp(jax.random.uniform(jax.random.fold_in(own, dim), (shards_of,), jnp.float32, least / len(split), largest / len(split)))
        factor_of = factor_of * jnp.repeat(draws, shape[dim] // shards_of).reshape([-1 if axis == dim else 1 for axis in range(len(shape))])
    return factor_of


def gaussian(rng, extent, spread, limit, cuts=(), kind=jnp.bfloat16):
    drawn = jax.random.normal(rng, extent, jnp.float32) * spread
    if len(cuts) > 0:
        drawn = levels(rng, extent, cuts, -0.22, 0.18) * drawn
    return jnp.clip(drawn, min=-limit, max=limit).astype(kind)


def setup_inputs(seed: int = 0) -> dict:
    keys = jax.random.split(jax.random.key(seed), 14)
    length = jax.random.randint(keys[0], (1,), PROMPT_TOKENS // 2, PROMPT_TOKENS + 1).astype(jnp.int32)
    mamba_in = gaussian(keys[1], (PROMPT_TOKENS, DI), 1.0, 6.0, ((0, 8), (1, 4)))
    gate_in = gaussian(keys[2], (PROMPT_TOKENS, DI), 1.0, 6.0, ((0, 8), (1, 4)))
    step_raw = gaussian(keys[3], (PROMPT_TOKENS, DI), 0.5, 3.0, ((0, 8), (1, 4)))
    conv_weight = gaussian(keys[4], (KW, DI), KW ** -0.5, 3.0, ((1, 4),), jnp.float32)
    conv_bias = gaussian(keys[5], (DI,), 0.5, 3.0, ((0, 4),), jnp.float32)
    step_bias = jnp.clip(jax.random.uniform(keys[6], (DI,), jnp.float32, -1.0, 1.0) * levels(keys[6], (DI,), ((0, 4),), -0.4, 0.0), -1.0, 1.0)
    decay_rates = jnp.clip(jnp.exp(math.log(0.04) - 6.7083282 * jax.random.uniform(keys[7], (NS, DI), jnp.float32) ** levels(keys[7], (NS, DI), ((1, 4),), -0.2, 0.2)), 4.882812572759576e-05, 0.04)
    skip_gain = jnp.clip(0.5 + 1.0 * jax.random.uniform(keys[8], (DI,), jnp.float32) ** levels(keys[8], (DI,), ((0, 4),), -0.2, 0.2), 0.5, 1.5)
    state_proj = gaussian(keys[9], (DI, 2 * NS), (DI * PROMPT_TOKENS // 64) ** -0.5, 0.015625, ((0, 4),))
    query_input_rows = draw_query_input_rows(jax.random.fold_in(keys[13], 71), 0)
    key_input_rows = draw_key_input_rows(jax.random.fold_in(keys[13], 71), 0)
    value_input_rows = gaussian(keys[12], (PROMPT_TOKENS, KEY_VALUE_HEADS * HEAD_WIDTH), 1.0, 6.0, ((0, 8), (1, 4)))
    return {"length": length, "mamba_in": mamba_in, "gate_in": gate_in, "step_raw": step_raw, "conv_weight": conv_weight, "conv_bias": conv_bias, "step_bias": step_bias, "decay_rates": decay_rates, "skip_gain": skip_gain, "state_proj": state_proj, "query_input_rows": query_input_rows, "key_input_rows": key_input_rows, "value_input_rows": value_input_rows}


def mamba_part(length, mamba_in, gate_in, step_raw, conv_weight, conv_bias, step_bias, decay_rates, skip_gain, state_proj):
    input_float = mamba_in.astype(jnp.float32)
    padded = jnp.concatenate([jnp.zeros((KW - 1, DI), jnp.float32), input_float], axis=0)
    convolved = jnp.broadcast_to(conv_bias[None, :], input_float.shape)
    for tap_index in range(KW):
        convolved = convolved + conv_weight[tap_index][None, :] * padded[tap_index:tap_index + PROMPT_TOKENS]
    conv_out = jax.nn.silu(convolved).astype(jnp.bfloat16)
    projected = jnp.dot(conv_out, state_proj, preferred_element_type=jnp.float32)
    inject = projected[:, :NS]
    readout = projected[:, NS:]
    positions = jnp.arange(PROMPT_TOKENS, dtype=jnp.int32)
    is_valid = (positions < length[0]).astype(jnp.float32)
    step_size = jax.nn.softplus(step_raw.astype(jnp.float32) + step_bias[None, :]) * is_valid[:, None]
    mixed_float = conv_out.astype(jnp.float32)

    def advance(state, inputs):
        step_now, inject_now, readout_now, mixed_step = inputs
        state = jnp.exp(-decay_rates * step_now[None, :]) * state + inject_now[:, None] * (step_now * mixed_step)[None, :]
        return (state, lax.optimization_barrier(jnp.sum(readout_now[:, None] * state, axis=0)))
    _, scanned = lax.scan(advance, jnp.zeros((NS, DI), jnp.float32), (step_size, inject, readout, mixed_float))
    mixed = (scanned + skip_gain[None, :] * mixed_float) * jax.nn.silu(gate_in.astype(jnp.float32))
    return mixed.astype(jnp.bfloat16)

def attention_part(length, query_input_rows, key_input_rows, value_input_rows):
    query_group_count = QUERY_HEADS // KEY_VALUE_HEADS
    query_head_rows = query_input_rows.reshape(PROMPT_TOKENS, KEY_VALUE_HEADS, query_group_count, HEAD_WIDTH)
    key_head_rows = key_input_rows.reshape(PROMPT_TOKENS, KEY_VALUE_HEADS, HEAD_WIDTH).astype(jnp.float32)
    value_head_rows = value_input_rows.reshape(PROMPT_TOKENS, KEY_VALUE_HEADS, HEAD_WIDTH).astype(jnp.float32)
    score_scale = 1.0 / math.sqrt(HEAD_WIDTH)
    query_block = math.gcd(PROMPT_TOKENS, 128)
    positions = jnp.arange(PROMPT_TOKENS, dtype=jnp.int32)
    key_valid = positions < length[0]

    def one_block(block_index):
        start = (block_index * query_block).astype(jnp.int32)
        block_queries = lax.dynamic_slice_in_dim(query_head_rows, start, query_block, 0).astype(jnp.float32)
        scores = jnp.einsum('qhgd,khd->qhgk', block_queries, key_head_rows, precision=lax.Precision.HIGHEST) * score_scale
        query_pos = start + jnp.arange(query_block, dtype=jnp.int32)
        allowed = (positions[None, :] <= query_pos[:, None]) & key_valid[None, :]
        scores = jnp.where(allowed[:, None, None, :], scores, -jnp.inf)
        highest = lax.optimization_barrier(jnp.max(scores, axis=-1))
        weights = jnp.exp(scores - highest[..., None])
        total = lax.optimization_barrier(jnp.sum(weights, axis=-1))
        rounded = lax.optimization_barrier(weights.astype(jnp.bfloat16)).astype(jnp.float32)
        summed = jnp.einsum('qhgk,khd->qhgd', rounded, value_head_rows, precision=lax.Precision.HIGHEST)
        return (summed / total[..., None]).astype(jnp.bfloat16)
    blocks = lax.map(one_block, jnp.arange(PROMPT_TOKENS // query_block, dtype=jnp.int32))
    return blocks.reshape(PROMPT_TOKENS, QUERY_HEADS * HEAD_WIDTH)

def reference(length, mamba_in, gate_in, step_raw, conv_weight, conv_bias, step_bias, decay_rates, skip_gain, state_proj, query_input_rows, key_input_rows, value_input_rows):
    mamba_out = mamba_part(length, mamba_in, gate_in, step_raw, conv_weight, conv_bias, step_bias, decay_rates, skip_gain, state_proj)
    attn_out = attention_part(length, query_input_rows, key_input_rows, value_input_rows)
    return (mamba_out, attn_out)
```

```python
import functools
import math

import jax
import jax.numpy as jnp
from jax import lax
from jax.experimental import pallas as pl
from jax.experimental.pallas import tpu as pltpu
from jax.sharding import PartitionSpec as P

KW = 4
HEAD_WIDTH = 128
LANES = 128
BLOCK = 16
WIDE = 512
TILE = 256
LOG2E = 1.4426950408889634
LOW = -1e30
MESH = pl.DeviceIdType.MESH
F32 = jnp.float32
BF16 = jnp.bfloat16


def each(count, body):
    if count <= 8:
        for i in range(count):
            body(i)
    else:
        @pl.loop(0, count)
        def _(i):
            body(i)


def silu(v):
    return v / (1.0 + jnp.exp(-v))


def block_rows(b, size):
    return pl.ds(pl.multiple_of(b * size, size), size)


def main_kernel(
    n_ctx, n_ten, group, own_lo, n_own,
    length_hbm, mamba_hbm, step_hbm, conv_w_hbm, step_b_hbm, rates_hbm, conv_b_hbm, proj_hbm, gate_hbm,
    keys_hbm, values_hbm, skip_hbm, query_hbm,
    gone_out, base_y, gate_out, inc_out, lhs, attn_out,
    length, mamba, step_raw, conv_w, step_b, rates, conv_b, proj, gate, skip, query,
    x_a, conv_out, step_a, driven, rate_s, rate_flat, sums_a, spread, decay_a, state_a, main_fin, early_fin,
    halo_f, halo_out, halo_in, part_all, e_all, s_out, s_in, p_out, p_in, kv_all, top, tot, acc,
    halo_send, halo_recv, part_send, part_recv, s_send, s_recv, p_send, p_recv, e_send, e_recv,
    kv_send, kv_recv, kv_forward, load_sem,
):
    tok, chans = mamba.shape
    ch = chans // LANES
    ns = rates.shape[0]
    blocks = tok // BLOCK
    pieces = s_out.shape[1]
    me = lax.axis_index("context")
    mt = lax.axis_index("tensor")

    def ctx_copy(src, dst, send, recv, to):
        return pltpu.make_async_remote_copy(
            src_ref=src, dst_ref=dst, send_sem=send, recv_sem=recv,
            device_id={"context": to}, device_id_type=MESH,
        )

    def others(body):
        each(n_ctx - 1, lambda d: body(lax.rem(me + d + 1, n_ctx)))

    barrier = pltpu.get_barrier_semaphore()
    for d in range(1, n_ten):
        pl.semaphore_signal(
            barrier, inc=1, device_id={"tensor": lax.rem(mt + d, n_ten)}, device_id_type=MESH
        )
    others(lambda to: pl.semaphore_signal(barrier, inc=1, device_id={"context": to}, device_id_type=MESH))

    sources = (
        mamba_hbm, step_hbm, length_hbm, conv_w_hbm, step_b_hbm, rates_hbm, conv_b_hbm, proj_hbm, gate_hbm,
        keys_hbm, values_hbm, skip_hbm, query_hbm,
    )
    targets = (
        mamba, step_raw, length, conv_w, step_b, rates, conv_b, proj, gate,
        kv_all.at[me, 0], kv_all.at[me, 1], skip, query,
    )
    loads = [
        pltpu.make_async_copy(src, dst, load_sem.at[i])
        for i, (src, dst) in enumerate(zip(sources, targets))
    ]
    for load in loads:
        load.start()

    first = me * tok
    for load in loads[:7]:
        load.wait()
    prompt_end = length[0]
    valid = (first + lax.broadcasted_iota(jnp.int32, (tok, LANES), 0)) < prompt_end
    conv_out[0:BLOCK, :] = jnp.zeros((BLOCK, chans), BF16)

    def convolve(g, lanes, start, count):
        total = jnp.broadcast_to(conv_b[pl.ds(g, 1), :], (count, LANES))
        for j in range(KW):
            at = 8 + start - (KW - 1) + j
            total = total + conv_w[j : j + 1, lanes] * x_a[g, at : at + count, :]
        mixed = silu(total).astype(BF16)
        conv_out[start : start + count, lanes] = mixed
        driven[start : start + count, lanes] = step_a[start : start + count, lanes] * mixed.astype(F32)

    @pl.loop(0, ch)
    def _(g):
        lanes = block_rows(g, LANES)
        x = mamba[:, lanes].astype(F32)
        x_a[g, 8 : 8 + tok, :] = x
        for j in range(KW - 1):
            at = tok - (KW - 1) + j
            halo_f[pl.ds(j * ch + g, 1), :] = x[at : at + 1, :]
        raw = step_raw[:, lanes].astype(F32) + step_b[pl.ds(g, 1), :]
        size = jnp.maximum(raw, 0.0) + jnp.log(1.0 + jnp.exp(-jnp.abs(raw)))
        size = jnp.where(valid, size, 0.0)
        step_a[:, lanes] = size
        early = jnp.sum(size[:BLOCK], axis=0, keepdims=True)
        late = jnp.sum(size[BLOCK:], axis=0, keepdims=True)
        sums_a[0:1, lanes] = early
        sums_a[1:2, lanes] = late
        e_all[me, pl.ds(g, 1), :] = early + late
        scaled = rates[:, lanes] * (-LOG2E)
        rate_s[:, lanes] = scaled
        rate_flat[block_rows(g, ns), :] = scaled
        convolve(g, lanes, BLOCK, tok - BLOCK)

    halo_out[...] = halo_f[...].astype(BF16)
    loads[7].wait()

    def partial_projection(count):
        return lax.dot_general(
            proj[...], conv_out[0:count, :], (((1,), (1,)), ((), ())), preferred_element_type=F32
        )

    part_all[0, mt] = partial_projection(tok)

    for load in loads[8:]:
        load.wait()

    @pl.loop(0, ch)
    def _(g):
        lanes = block_rows(g, LANES)
        gate_out[:, lanes] = silu(gate[:, lanes].astype(F32))

    pl.semaphore_wait(barrier, n_ctx - 1 + n_ten - 1)

    halo = ctx_copy(halo_out, halo_in, halo_send, halo_recv, lax.rem(me + 1, n_ctx))

    @pl.when(me < n_ctx - 1)
    def _():
        halo.start()

    def part_copy(late, src, to):
        return pltpu.make_async_remote_copy(
            src_ref=part_all.at[late, src], dst_ref=part_all.at[late, src],
            send_sem=part_send.at[late, to], recv_sem=part_recv.at[late, src],
            device_id={"tensor": to}, device_id_type=MESH,
        )

    def peers(body):
        for d in range(1, n_ten):
            body(lax.rem(mt + d, n_ten))

    peers(lambda to: part_copy(0, mt, to).start())

    def owners(body):
        def visit(o):
            to = own_lo + o

            @pl.when(to != me)
            def _():
                body(o, to)

        each(n_own, visit)

    is_owner = jnp.logical_and(me >= own_lo, me < own_lo + n_own)

    def e_copy(src, to, slot):
        return ctx_copy(e_all.at[src], e_all.at[src], e_send.at[slot], e_recv.at[src], to)

    @pl.when(me < n_ctx - 1)
    def _():
        owners(lambda o, to: e_copy(me, to, o).start())

    twin = me + 1 - 2 * lax.rem(me, 2)
    steps = n_ctx // 2 - 1

    def kv_copy(src, to, send):
        return ctx_copy(kv_all.at[src], kv_all.at[src], send, kv_recv.at[src], to)

    def kv_line(body):
        def visit(d):
            to = me + 2 * (d + 1)

            @pl.when(to < n_ctx)
            def _():
                body(to)

        each(n_ctx // 2 - 1, visit)

        @pl.when(lax.rem(me, 2) == 0)
        def _():
            body(me + 1)

    kv_line(lambda to: kv_copy(me, to, kv_send.at[to]).start())

    def forward(d):
        src = me - 2 * (d + 1)

        @pl.when(src >= 0)
        def _():
            kv_copy(src, twin, kv_forward.at[src]).wait_recv()
            kv_copy(src, twin, kv_forward.at[src]).start()

    def row(ref, t, cols):
        return jnp.broadcast_to(ref[pl.ds(t, 1), cols], (ns, WIDE))

    chunks = [slice(q * WIDE, (q + 1) * WIDE) for q in range(chans // WIDE)]
    for cols in chunks:
        rate = rate_s[:, cols]

        @pl.loop(0, blocks)
        def _(b):
            for k in range(BLOCK):
                t = b * BLOCK + k
                decay_a[block_rows(t, ns), cols] = jnp.exp2(rate * row(step_a, t, cols))

    @pl.when(me > 0)
    def _():
        halo.wait_recv()
        halo_f[...] = halo_in[...].astype(F32)

    @pl.when(me == 0)
    def _():
        halo_f[...] = jnp.zeros_like(halo_f)

    @pl.loop(0, ch)
    def _(g):
        for j in range(KW - 1):
            at = 8 - (KW - 1) + j
            x_a[g, at : at + 1, :] = halo_f[pl.ds(j * ch + g, 1), :]
        convolve(g, block_rows(g, LANES), 0, BLOCK)

    part_all[1, mt] = jnp.concatenate(
        [partial_projection(BLOCK), jnp.zeros((2 * ns, tok - BLOCK), F32)], axis=1
    )
    peers(lambda to: part_copy(1, mt, to).start())

    def collect(late, start, stop):
        peers(lambda src: part_copy(late, src, mt).wait_recv())
        projected = part_all[late, 0]
        for d in range(1, n_ten):
            projected = projected + part_all[late, d]
        for t in range(start, stop):
            spread[t * ns : (t + 1) * ns, :] = jnp.broadcast_to(projected[:ns, t : t + 1], (ns, LANES))
        source = lax.broadcasted_iota(jnp.int32, (2 * ns, BLOCK * ns), 0) - ns
        entry = lax.rem(lax.broadcasted_iota(jnp.int32, (2 * ns, BLOCK * ns), 1), ns)
        pick = jnp.where(source == entry, 1.0, 0.0).astype(BF16)
        rows = projected.T[start:stop].astype(BF16)
        wide = jnp.dot(rows, pick, preferred_element_type=F32)
        token = lax.rem(lax.broadcasted_iota(jnp.int32, wide.shape, 0), BLOCK)
        owner = lax.broadcasted_iota(jnp.int32, wide.shape, 1) // ns
        lhs[start:stop, :] = jnp.where(token == owner, wide, 0.0).astype(BF16)

    collect(0, BLOCK, tok)

    def advance(b, state, cols):
        for k in range(BLOCK):
            t = b * BLOCK + k
            rows = block_rows(t, ns)
            inject = jnp.concatenate([spread[rows, :]] * (WIDE // LANES), axis=1)
            state = decay_a[rows, cols] * state + inject * row(driven, t, cols)
            state_a[rows, cols] = state.astype(BF16)
        return state

    for cols in chunks:
        main_fin[:, cols] = lax.fori_loop(
            1, blocks, lambda b, state: advance(b, state, cols), jnp.zeros((ns, WIDE), F32)
        )

    collect(1, 0, BLOCK)

    def s_copy(o, src, to):
        return ctx_copy(s_out.at[o], s_in.at[src], s_send.at[o], s_recv.at[src], to)

    share = n_own // len(chunks)
    for q, cols in enumerate(chunks):
        early = advance(0, jnp.zeros((ns, WIDE), F32), cols)
        early_fin[:, cols] = early
        final = main_fin[:, cols] + jnp.exp2(rate_s[:, cols] * sums_a[1:2, cols]) * early
        flat = jnp.concatenate([final[:, k * LANES : (k + 1) * LANES] for k in range(WIDE // LANES)], axis=0)
        s_out[q * share : (q + 1) * share] = flat.astype(s_out.dtype).reshape(share, pieces, LANES)

        def send(i):
            o = q * share + i
            to = own_lo + o

            @pl.when(jnp.logical_and(to != me, me < n_ctx - 1))
            def _():
                s_copy(o, me, to).start()

        each(share, send)

    each(steps, forward)

    for cols in chunks:
        def shrink(b, gone):
            for k in range(BLOCK):
                rows = block_rows(b * BLOCK + k, ns)
                gone = gone * decay_a[rows, cols]
                gone_out[rows, cols] = gone.astype(BF16)
            return gone

        shrink(0, jnp.ones((ns, WIDE), F32))
        lax.fori_loop(1, blocks, shrink, jnp.ones((ns, WIDE), F32))

    for q in range(chans // TILE):
        cols = slice(q * TILE, (q + 1) * TILE)
        gain = jnp.concatenate(
            [skip[g : g + 1, :] for g in range(q * TILE // LANES, (q + 1) * TILE // LANES)], axis=1
        )

        @pl.loop(0, blocks)
        def _(b):
            rows = block_rows(b, BLOCK)
            base_y[rows, cols] = gain * conv_out[rows, cols].astype(F32) + jnp.dot(
                lhs[rows, :], state_a[block_rows(b, BLOCK * ns), cols], preferred_element_type=F32
            )

    def p_copy(k, o, to):
        return ctx_copy(p_out.at[k], p_in.at[o], p_send.at[k], p_recv.at[o], to)

    @pl.when(is_owner)
    def _():
        o = me - own_lo
        s_in[me] = s_out[o]
        my_rate = rate_flat[pl.ds(o * pieces, pieces), :]

        def arrive(j):
            @pl.when(j != me)
            def _():
                e_copy(j, me, 0).wait_recv()
                s_copy(0, j, me).wait_recv()

        each(n_ctx - 1, arrive)

        def fold(j, running):
            p_out[j] = running.astype(p_out.dtype)
            if pieces >= ns:
                count = pieces // ns
                gone = jnp.concatenate(
                    [
                        jnp.broadcast_to(e_all[j, pl.ds(o * count + i, 1), :], (ns, LANES))
                        for i in range(count)
                    ],
                    axis=0,
                )
            else:
                gone = jnp.broadcast_to(e_all[j, pl.ds(o * pieces // ns, 1), :], (pieces, LANES))
            return jnp.exp2(my_rate * gone) * running + s_in[j].astype(F32)

        running = jnp.zeros((pieces, LANES), F32)
        if n_ctx <= 8:
            for j in range(n_ctx - 1):
                running = fold(j, running)
        else:
            running = lax.fori_loop(0, n_ctx - 1, fold, running)
        p_out[n_ctx - 1] = running.astype(p_out.dtype)

        def send(k):
            @pl.when(k + 1 != me)
            def _():
                p_copy(k + 1, o, k + 1).start()

        each(n_ctx - 1, send)
        p_in[o] = p_out[me]

    def arrive(d):
        src = twin - 2 * (d + 1)

        @pl.when(src >= 0)
        def _():
            kv_copy(src, twin, kv_send.at[src]).wait_recv()

    each(steps, arrive)

    @pl.when(lax.rem(me, 2) == 1)
    def _():
        kv_copy(me - 1, twin, kv_send.at[0]).wait_recv()

    scale = LOG2E / math.sqrt(HEAD_WIDTH)
    heads = query.shape[1] // HEAD_WIDTH
    row_pos = first + lax.broadcasted_iota(jnp.int32, (tok, tok), 0)
    last_key = jnp.minimum(row_pos, prompt_end - 1)
    key_iota = lax.broadcasted_iota(jnp.int32, (tok, tok), 1)
    across = decay_a.shape[0] // tok

    def slot(j, g):
        i = j * group + g
        return block_rows(lax.rem(i, across), tok), block_rows(i // across, LANES)

    def attend(head0):
        top[...] = jnp.full(top.shape, LOW, F32)
        tot[...] = jnp.zeros(tot.shape, F32)
        acc[...] = jnp.zeros(acc.shape, F32)

        @pl.loop(0, me + 1)
        def _(j):
            block = kv_all[j, 0]
            allowed = (key_iota + j * tok) <= last_key
            for g in range(group):
                cols = slice((head0 + g) * HEAD_WIDTH, (head0 + g + 1) * HEAD_WIDTH)
                s = lax.dot_general(
                    query[:, cols], block, (((1,), (1,)), ((), ())), preferred_element_type=F32
                )
                s = jnp.where(allowed, s, LOW)
                top[g] = jnp.maximum(top[g], s)
                rows, lanes = slot(j, g)
                decay_a[rows, lanes] = s

        highest = [jnp.max(top[g], axis=1, keepdims=True) for g in range(group)]
        for g in range(group):
            top[g] = jnp.broadcast_to(highest[g], (tok, tok))

        @pl.loop(0, me + 1)
        def _(j):
            block = kv_all[j, 1]
            for g in range(group):
                rows, lanes = slot(j, g)
                w = jnp.exp2((decay_a[rows, lanes] - top[g]) * scale)
                tot[g] = tot[g] + w
                acc[g] = acc[g] + jnp.dot(w.astype(BF16), block, preferred_element_type=F32)

        for g in range(group):
            cols = slice((head0 + g) * HEAD_WIDTH, (head0 + g + 1) * HEAD_WIDTH)
            total = jnp.sum(tot[g], axis=1, keepdims=True)
            attn_out[:, cols] = (acc[g] / total).astype(BF16)

    for head0 in range(0, heads, group):
        attend(head0)

    @pl.when(me > 0)
    def _():
        owners(lambda o, to: p_copy(0, o, me).wait_recv())

    @pl.when(me == 0)
    def _():
        p_in[...] = jnp.zeros_like(p_in)

    entering = p_in[...].reshape(ns * ch, LANES).astype(F32)
    for g in range(ch):
        lanes = slice(g * LANES, (g + 1) * LANES)
        now = entering[g * ns : (g + 1) * ns, :]
        inc_out[0, :, lanes] = now.astype(BF16)
        later = early_fin[:, lanes] + jnp.exp2(rate_s[:, lanes] * sums_a[0:1, lanes]) * now
        inc_out[1, :, lanes] = later.astype(BF16)

    @pl.when(me < n_ctx - 1)
    def _():
        halo.wait_send()
        owners(lambda o, to: e_copy(me, to, o).wait_send())
        owners(lambda o, to: s_copy(o, me, to).wait_send())

    for late in range(2):
        peers(lambda to: part_copy(late, mt, to).wait_send())
    kv_line(lambda to: kv_copy(me, to, kv_send.at[to]).wait_send())

    def end_forward(d):
        src = me - 2 * (d + 1)

        @pl.when(src >= 0)
        def _():
            kv_copy(src, twin, kv_forward.at[src]).wait_send()

    each(steps, end_forward)

    @pl.when(is_owner)
    def _():
        def sent(k):
            @pl.when(k + 1 != me)
            def _():
                p_copy(k + 1, 0, k + 1).wait_send()

        each(n_ctx - 1, sent)


def last_kernel(
    gone, base_y, gate, inc, lhs, attn, mamba_out_hbm, attn_out_hbm, out, attn_sem, out_sem
):
    tok, chans = base_y.shape
    ns = inc.shape[1]
    attn_store = pltpu.make_async_copy(attn, attn_out_hbm, attn_sem)
    attn_store.start()
    stores = []
    for q in range(chans // TILE):
        cols = slice(q * TILE, (q + 1) * TILE)
        for b in range(tok // BLOCK):
            rows = slice(b * BLOCK, (b + 1) * BLOCK)
            held = gone[b * BLOCK * ns : (b + 1) * BLOCK * ns, cols].reshape(BLOCK, ns, TILE)
            held = (held * inc[min(b, 1), :, cols][None]).reshape(BLOCK * ns, TILE)
            y = base_y[rows, cols] + jnp.dot(lhs[rows, :], held, preferred_element_type=F32)
            out[rows, cols] = (y * gate[rows, cols]).astype(BF16)
        stores.append(pltpu.make_async_copy(out.at[:, cols], mamba_out_hbm.at[:, cols], out_sem.at[q]))
        stores[-1].start()
    attn_store.wait()
    for store in stores:
        store.wait()


def shards(
    n_ctx, n_ten,
    length, mamba_in, gate_in, step_raw, conv_weight, conv_bias, step_bias, decay_rates, skip_gain,
    state_proj, query_input_rows, key_input_rows, value_input_rows,
):
    tok, chans = mamba_in.shape
    ch = chans // LANES
    ns = decay_rates.shape[0]
    heads = query_input_rows.shape[1] // HEAD_WIDTH
    group = heads // 2
    while group > 1 and n_ctx * group * tok * LANES > tok * ns * chans:
        group //= 2
    own_lo, n_own = n_ctx // 4, n_ctx // 2
    pieces = ns * ch // n_own
    link = BF16 if pieces % 16 == 0 else F32
    dma = pltpu.SemaphoreType.DMA
    hbm = pl.BlockSpec(memory_space=pl.ANY)
    vmem = pl.BlockSpec(memory_space=pltpu.VMEM)
    ordered = (
        length, mamba_in, step_raw, conv_weight, step_bias.reshape(ch, LANES), decay_rates,
        conv_bias.reshape(ch, LANES), state_proj.T, gate_in, key_input_rows, value_input_rows,
        skip_gain.reshape(ch, LANES), query_input_rows,
    )
    held = [pltpu.SMEM((1,), jnp.int32)]
    held += [pltpu.VMEM(a.shape, a.dtype) for i, a in enumerate(ordered) if i not in (0, 9, 10)]
    channels = pltpu.VMEM((ns, chans), F32)
    halo = ((KW - 1) * ch, LANES)
    parts = pl.pallas_call(
        functools.partial(main_kernel, n_ctx, n_ten, group, own_lo, n_own),
        out_shape=(
            pltpu.VMEM((tok * ns, chans), BF16),
            pltpu.VMEM((tok, chans), F32),
            pltpu.VMEM((tok, chans), F32),
            pltpu.VMEM((2, ns, chans), BF16),
            pltpu.VMEM((tok, BLOCK * ns), BF16),
            pltpu.VMEM(query_input_rows.shape, BF16),
        ),
        in_specs=[hbm] * 13,
        out_specs=(vmem,) * 6,
        scratch_shapes=held + [
            pltpu.VMEM((ch, tok + 8, LANES), F32),
            pltpu.VMEM((tok, chans), BF16),
            pltpu.VMEM((tok, chans), F32),
            pltpu.VMEM((tok, chans), F32),
            channels,
            pltpu.VMEM((ns * ch, LANES), F32),
            pltpu.VMEM((2, chans), F32),
            pltpu.VMEM((tok * ns, LANES), F32),
            pltpu.VMEM((tok * ns, chans), F32),
            pltpu.VMEM((tok * ns, chans), BF16),
            channels,
            channels,
            pltpu.VMEM(halo, F32), pltpu.VMEM(halo, BF16), pltpu.VMEM(halo, BF16),
            pltpu.VMEM((2, n_ten, 2 * ns, tok), F32),
            pltpu.VMEM((n_ctx, ch, LANES), F32),
            pltpu.VMEM((n_own, pieces, LANES), link),
            pltpu.VMEM((n_ctx, pieces, LANES), link),
            pltpu.VMEM((n_ctx, pieces, LANES), link),
            pltpu.VMEM((n_own, pieces, LANES), link),
            pltpu.VMEM((n_ctx, 2, tok, HEAD_WIDTH), BF16),
            pltpu.VMEM((group, tok, tok), F32),
            pltpu.VMEM((group, tok, tok), F32),
            pltpu.VMEM((group, tok, HEAD_WIDTH), F32),
            dma, dma, dma((2, n_ten)), dma((2, n_ten)),
            dma((n_own,)), dma((n_ctx,)), dma((n_ctx,)), dma((n_own,)),
            dma((n_own,)), dma((n_ctx,)), dma((n_ctx,)), dma((n_ctx,)), dma((n_ctx,)),
            dma((len(ordered),)),
        ],
        compiler_params=pltpu.CompilerParams(
            collective_id=0, has_side_effects=True, vmem_limit_bytes=48 << 20
        ),
    )(*ordered)
    return pl.pallas_call(
        last_kernel,
        out_shape=(
            jax.ShapeDtypeStruct(mamba_in.shape, BF16),
            jax.ShapeDtypeStruct(query_input_rows.shape, BF16),
        ),
        in_specs=[vmem] * 6,
        out_specs=(hbm, hbm),
        scratch_shapes=[pltpu.VMEM((tok, chans), BF16), dma, dma((chans // TILE,))],
        compiler_params=pltpu.CompilerParams(vmem_limit_bytes=16 << 20),
    )(*parts)


def solution(mesh):
    both = P("context", "tensor")
    in_specs = (
        P(), both, both, both, P(None, "tensor"), P("tensor"), P("tensor"), P(None, "tensor"),
        P("tensor"), P("tensor", None), both, both, both,
    )
    body = functools.partial(shards, mesh.shape["context"], mesh.shape["tensor"])
    return jax.shard_map(body, mesh=mesh, in_specs=in_specs, out_specs=(both, both), check_vma=False)
```

```python
import functools
import math

import jax
import jax.numpy as jnp
from jax import lax
from jax.experimental import pallas as pl
from jax.experimental.pallas import tpu as pltpu
from jax.sharding import PartitionSpec as P

KW = 4
HEAD_WIDTH = 128
LANES = 128
BLOCK = 16
WIDE = 512
TILE = 256
LOG2E = 1.4426950408889634
LOW = -1e30
MESH = pl.DeviceIdType.MESH
F32 = jnp.float32
BF16 = jnp.bfloat16


def each(count, body):
    if count <= 8:
        for i in range(count):
            body(i)
    else:
        @pl.loop(0, count)
        def _(i):
            body(i)


def silu(v):
    return v / (1.0 + jnp.exp(-v))


def block_rows(b, size):
    return pl.ds(pl.multiple_of(b * size, size), size)


def main_kernel(
    n_ctx, n_ten, group, own_lo, n_own,
    length_hbm, mamba_hbm, step_hbm, conv_w_hbm, step_b_hbm, rates_hbm, conv_b_hbm, proj_hbm, gate_hbm,
    keys_hbm, values_hbm, skip_hbm, query_hbm,
    gone_out, base_y, gate_out, inc_out, lhs, attn_out,
    length, mamba, step_raw, conv_w, step_b, rates, conv_b, proj, gate, skip, query,
    x_a, conv_out, step_a, driven, rate_s, rate_flat, sums_a, spread, decay_a, state_a, main_fin, early_fin,
    halo_f, halo_out, halo_in, part_all, e_all, s_out, s_in, p_out, p_in, kv_all, top, own_scores, acc,
    halo_send, halo_recv, part_send, part_recv, s_send, s_recv, p_send, p_recv, e_send, e_recv,
    kv_send, kv_recv, kv_forward, load_sem,
):
    tok, chans = mamba.shape
    ch = chans // LANES
    ns = rates.shape[0]
    blocks = tok // BLOCK
    pieces = s_out.shape[1]
    me = lax.axis_index("context")
    mt = lax.axis_index("tensor")

    def ctx_copy(src, dst, send, recv, to):
        return pltpu.make_async_remote_copy(
            src_ref=src, dst_ref=dst, send_sem=send, recv_sem=recv,
            device_id={"context": to}, device_id_type=MESH,
        )

    def others(body):
        each(n_ctx - 1, lambda d: body(lax.rem(me + d + 1, n_ctx)))

    barrier = pltpu.get_barrier_semaphore()
    for d in range(1, n_ten):
        pl.semaphore_signal(
            barrier, inc=1, device_id={"tensor": lax.rem(mt + d, n_ten)}, device_id_type=MESH
        )
    others(lambda to: pl.semaphore_signal(barrier, inc=1, device_id={"context": to}, device_id_type=MESH))

    sources = (
        mamba_hbm, step_hbm, length_hbm, conv_w_hbm, step_b_hbm, rates_hbm, conv_b_hbm, proj_hbm, gate_hbm,
        keys_hbm, values_hbm, skip_hbm, query_hbm,
    )
    targets = (
        mamba, step_raw, length, conv_w, step_b, rates, conv_b, proj, gate,
        kv_all.at[me, 0], kv_all.at[me, 1], skip, query,
    )
    loads = [
        pltpu.make_async_copy(src, dst, load_sem.at[i])
        for i, (src, dst) in enumerate(zip(sources, targets))
    ]
    for load in loads:
        load.start()

    first = me * tok
    for load in loads[:7]:
        load.wait()
    prompt_end = length[0]
    valid = (first + lax.broadcasted_iota(jnp.int32, (tok, LANES), 0)) < prompt_end
    conv_out[0:BLOCK, :] = jnp.zeros((BLOCK, chans), BF16)

    def convolve(g, lanes, start, count):
        total = jnp.broadcast_to(conv_b[pl.ds(g, 1), :], (count, LANES))
        for j in range(KW):
            at = 8 + start - (KW - 1) + j
            total = total + conv_w[j : j + 1, lanes] * x_a[g, at : at + count, :]
        mixed = silu(total).astype(BF16)
        conv_out[start : start + count, lanes] = mixed
        driven[start : start + count, lanes] = step_a[start : start + count, lanes] * mixed.astype(F32)

    @pl.loop(0, ch)
    def _(g):
        lanes = block_rows(g, LANES)
        x = mamba[:, lanes].astype(F32)
        x_a[g, 8 : 8 + tok, :] = x
        for j in range(KW - 1):
            at = tok - (KW - 1) + j
            halo_f[pl.ds(j * ch + g, 1), :] = x[at : at + 1, :]
        raw = step_raw[:, lanes].astype(F32) + step_b[pl.ds(g, 1), :]
        size = jnp.maximum(raw, 0.0) + jnp.log(1.0 + jnp.exp(-jnp.abs(raw)))
        size = jnp.where(valid, size, 0.0)
        step_a[:, lanes] = size
        early = jnp.sum(size[:BLOCK], axis=0, keepdims=True)
        late = jnp.sum(size[BLOCK:], axis=0, keepdims=True)
        sums_a[0:1, lanes] = early
        sums_a[1:2, lanes] = late
        e_all[me, pl.ds(g, 1), :] = early + late
        scaled = rates[:, lanes] * (-LOG2E)
        rate_s[:, lanes] = scaled
        rate_flat[block_rows(g, ns), :] = scaled
        convolve(g, lanes, BLOCK, tok - BLOCK)

    halo_out[...] = halo_f[...].astype(BF16)
    loads[7].wait()

    def partial_projection(count):
        return lax.dot_general(
            proj[...], conv_out[0:count, :], (((1,), (1,)), ((), ())), preferred_element_type=F32
        )

    part_all[0, mt] = partial_projection(tok)

    for load in loads[8:]:
        load.wait()

    @pl.loop(0, ch)
    def _(g):
        lanes = block_rows(g, LANES)
        gate_out[:, lanes] = silu(gate[:, lanes].astype(F32))

    pl.semaphore_wait(barrier, n_ctx - 1 + n_ten - 1)

    halo = ctx_copy(halo_out, halo_in, halo_send, halo_recv, lax.rem(me + 1, n_ctx))

    @pl.when(me < n_ctx - 1)
    def _():
        halo.start()

    def part_copy(late, src, to):
        return pltpu.make_async_remote_copy(
            src_ref=part_all.at[late, src], dst_ref=part_all.at[late, src],
            send_sem=part_send.at[late, to], recv_sem=part_recv.at[late, src],
            device_id={"tensor": to}, device_id_type=MESH,
        )

    def peers(body):
        for d in range(1, n_ten):
            body(lax.rem(mt + d, n_ten))

    peers(lambda to: part_copy(0, mt, to).start())

    def owners(body):
        def visit(o):
            to = own_lo + o

            @pl.when(to != me)
            def _():
                body(o, to)

        each(n_own, visit)

    is_owner = jnp.logical_and(me >= own_lo, me < own_lo + n_own)

    def e_copy(src, to, slot):
        return ctx_copy(e_all.at[src], e_all.at[src], e_send.at[slot], e_recv.at[src], to)

    @pl.when(me < n_ctx - 1)
    def _():
        owners(lambda o, to: e_copy(me, to, o).start())

    twin = me + 1 - 2 * lax.rem(me, 2)
    steps = n_ctx // 2 - 1

    def kv_copy(src, to, send):
        return ctx_copy(kv_all.at[src], kv_all.at[src], send, kv_recv.at[src], to)

    def kv_line(body):
        def visit(d):
            to = me + 2 * (d + 1)

            @pl.when(to < n_ctx)
            def _():
                body(to)

        each(n_ctx // 2 - 1, visit)

        @pl.when(lax.rem(me, 2) == 0)
        def _():
            body(me + 1)

    kv_line(lambda to: kv_copy(me, to, kv_send.at[to]).start())

    def forward(d):
        src = me - 2 * (d + 1)

        @pl.when(src >= 0)
        def _():
            kv_copy(src, twin, kv_forward.at[src]).wait_recv()
            kv_copy(src, twin, kv_forward.at[src]).start()

    def row(ref, t, cols):
        return jnp.broadcast_to(ref[pl.ds(t, 1), cols], (ns, WIDE))

    chunks = [slice(q * WIDE, (q + 1) * WIDE) for q in range(chans // WIDE)]
    for cols in chunks:
        rate = rate_s[:, cols]

        @pl.loop(0, blocks)
        def _(b):
            for k in range(BLOCK):
                t = b * BLOCK + k
                decay_a[block_rows(t, ns), cols] = jnp.exp2(rate * row(step_a, t, cols))

    @pl.when(me > 0)
    def _():
        halo.wait_recv()
        halo_f[...] = halo_in[...].astype(F32)

    @pl.when(me == 0)
    def _():
        halo_f[...] = jnp.zeros_like(halo_f)

    @pl.loop(0, ch)
    def _(g):
        for j in range(KW - 1):
            at = 8 - (KW - 1) + j
            x_a[g, at : at + 1, :] = halo_f[pl.ds(j * ch + g, 1), :]
        convolve(g, block_rows(g, LANES), 0, BLOCK)

    part_all[1, mt] = jnp.concatenate(
        [partial_projection(BLOCK), jnp.zeros((2 * ns, tok - BLOCK), F32)], axis=1
    )
    peers(lambda to: part_copy(1, mt, to).start())

    def collect(late, start, stop):
        peers(lambda src: part_copy(late, src, mt).wait_recv())
        projected = part_all[late, 0]
        for d in range(1, n_ten):
            projected = projected + part_all[late, d]
        for t in range(start, stop):
            spread[t * ns : (t + 1) * ns, :] = jnp.broadcast_to(projected[:ns, t : t + 1], (ns, LANES))
        source = lax.broadcasted_iota(jnp.int32, (2 * ns, BLOCK * ns), 0) - ns
        entry = lax.rem(lax.broadcasted_iota(jnp.int32, (2 * ns, BLOCK * ns), 1), ns)
        pick = jnp.where(source == entry, 1.0, 0.0).astype(BF16)
        rows = projected.T[start:stop].astype(BF16)
        wide = jnp.dot(rows, pick, preferred_element_type=F32)
        token = lax.rem(lax.broadcasted_iota(jnp.int32, wide.shape, 0), BLOCK)
        owner = lax.broadcasted_iota(jnp.int32, wide.shape, 1) // ns
        lhs[start:stop, :] = jnp.where(token == owner, wide, 0.0).astype(BF16)

    collect(0, BLOCK, tok)

    def advance(b, state, cols):
        for k in range(BLOCK):
            t = b * BLOCK + k
            rows = block_rows(t, ns)
            inject = jnp.concatenate([spread[rows, :]] * (WIDE // LANES), axis=1)
            state = decay_a[rows, cols] * state + inject * row(driven, t, cols)
            state_a[rows, cols] = state.astype(BF16)
        return state

    for cols in chunks:
        main_fin[:, cols] = lax.fori_loop(
            1, blocks, lambda b, state: advance(b, state, cols), jnp.zeros((ns, WIDE), F32)
        )

    collect(1, 0, BLOCK)

    def s_copy(o, src, to):
        return ctx_copy(s_out.at[o], s_in.at[src], s_send.at[o], s_recv.at[src], to)

    share = n_own // len(chunks)
    for q, cols in enumerate(chunks):
        early = advance(0, jnp.zeros((ns, WIDE), F32), cols)
        early_fin[:, cols] = early
        final = main_fin[:, cols] + jnp.exp2(rate_s[:, cols] * sums_a[1:2, cols]) * early
        flat = jnp.concatenate([final[:, k * LANES : (k + 1) * LANES] for k in range(WIDE // LANES)], axis=0)
        s_out[q * share : (q + 1) * share] = flat.astype(s_out.dtype).reshape(share, pieces, LANES)

        def send(i):
            o = q * share + i
            to = own_lo + o

            @pl.when(jnp.logical_and(to != me, me < n_ctx - 1))
            def _():
                s_copy(o, me, to).start()

        each(share, send)

    each(steps, forward)

    for cols in chunks:
        def shrink(b, gone):
            for k in range(BLOCK):
                rows = block_rows(b * BLOCK + k, ns)
                gone = gone * decay_a[rows, cols]
                gone_out[rows, cols] = gone.astype(BF16)
            return gone

        shrink(0, jnp.ones((ns, WIDE), F32))
        lax.fori_loop(1, blocks, shrink, jnp.ones((ns, WIDE), F32))

    @pl.loop(0, blocks)
    def _(b):
        rows = block_rows(b, BLOCK)
        left = lhs[rows, :]
        for q in range(chans // TILE):
            cols = slice(q * TILE, (q + 1) * TILE)
            gain = jnp.concatenate(
                [skip[g : g + 1, :] for g in range(q * TILE // LANES, (q + 1) * TILE // LANES)], axis=1
            )
            base_y[rows, cols] = gain * conv_out[rows, cols].astype(F32) + jnp.dot(
                left, state_a[block_rows(b, BLOCK * ns), cols], preferred_element_type=F32
            )

    def p_copy(k, o, to):
        return ctx_copy(p_out.at[k], p_in.at[o], p_send.at[k], p_recv.at[o], to)

    @pl.when(is_owner)
    def _():
        o = me - own_lo
        s_in[me] = s_out[o]
        my_rate = rate_flat[pl.ds(o * pieces, pieces), :]

        def arrive(j):
            @pl.when(j != me)
            def _():
                e_copy(j, me, 0).wait_recv()
                s_copy(0, j, me).wait_recv()

        each(n_ctx - 1, arrive)

        def fold(j, running):
            p_out[j] = running.astype(p_out.dtype)
            if pieces >= ns:
                count = pieces // ns
                gone = jnp.concatenate(
                    [
                        jnp.broadcast_to(e_all[j, pl.ds(o * count + i, 1), :], (ns, LANES))
                        for i in range(count)
                    ],
                    axis=0,
                )
            else:
                gone = jnp.broadcast_to(e_all[j, pl.ds(o * pieces // ns, 1), :], (pieces, LANES))
            return jnp.exp2(my_rate * gone) * running + s_in[j].astype(F32)

        running = jnp.zeros((pieces, LANES), F32)
        if n_ctx <= 8:
            for j in range(n_ctx - 1):
                running = fold(j, running)
        else:
            running = lax.fori_loop(0, n_ctx - 1, fold, running)
        p_out[n_ctx - 1] = running.astype(p_out.dtype)

        def send(k):
            @pl.when(k + 1 != me)
            def _():
                p_copy(k + 1, o, k + 1).start()

        each(n_ctx - 1, send)
        p_in[o] = p_out[me]

    def arrive(d):
        src = twin - 2 * (d + 1)

        @pl.when(src >= 0)
        def _():
            kv_copy(src, twin, kv_send.at[src]).wait_recv()

    each(steps, arrive)

    @pl.when(lax.rem(me, 2) == 1)
    def _():
        kv_copy(me - 1, twin, kv_send.at[0]).wait_recv()

    scale = LOG2E / math.sqrt(HEAD_WIDTH)
    heads = query.shape[1] // HEAD_WIDTH
    high = group * tok
    bands = decay_a.shape[0] // high
    pairs = (me + 1) // 2
    key_end = jnp.minimum(prompt_end, first)
    diagonal_iota = lax.broadcasted_iota(jnp.int32, (tok, tok), 1)
    allowed = jnp.logical_and(
        diagonal_iota <= lax.broadcasted_iota(jnp.int32, (tok, tok), 0), diagonal_iota + first < prompt_end
    )

    def known(p):
        return lax.broadcasted_iota(jnp.int32, (2 * tok, HEAD_WIDTH), 0) + p * (2 * tok) < key_end

    def both_blocks(p, what):
        return jnp.concatenate([kv_all[2 * p, what], kv_all[2 * p + 1, what]], axis=0).astype(F32)

    def scores_at(p):
        return lax.rem(p, bands) * high, block_rows(p // bands, 2 * tok)

    def dot_keys(q, keys):
        return lax.dot_general(q, keys, (((1,), (1,)), ((), ())), preferred_element_type=F32)

    def attend(head0):
        def span(g):
            return slice((head0 + g) * HEAD_WIDTH, (head0 + g + 1) * HEAD_WIDTH)

        def inner(g):
            return slice(g * tok, (g + 1) * tok)

        own_keys = kv_all[me, 0]
        for g in range(group):
            s = jnp.where(allowed, dot_keys(query[:, span(g)], own_keys), LOW)
            own_scores[inner(g), :] = s
            top[inner(g), :] = s

        @pl.loop(0, pairs)
        def _(p):
            stand_in = jnp.broadcast_to(kv_all[0, 0, 0:1, :].astype(F32), (2 * tok, HEAD_WIDTH))
            keys = jnp.where(known(p), both_blocks(p, 0), stand_in).astype(BF16)
            base, lanes = scores_at(p)
            for g in range(group):
                s = dot_keys(query[:, span(g)], keys)
                decay_a[pl.ds(pl.multiple_of(base + g * tok, tok), tok), lanes] = s
                top[inner(g), :] = jnp.maximum(top[inner(g), :], jnp.maximum(s[:, :tok], s[:, tok:]))

        own_values = jnp.concatenate([kv_all[me, 1], jnp.ones((tok, HEAD_WIDTH), BF16)], axis=1)
        for g in range(group):
            highest = jnp.broadcast_to(jnp.max(top[inner(g), :], axis=1, keepdims=True), (tok, tok))
            top[inner(g), :] = highest
            w = jnp.exp2((own_scores[inner(g), :] - highest) * scale).astype(BF16)
            acc[inner(g), :] = jnp.dot(w, own_values, preferred_element_type=F32)

        @pl.loop(0, pairs)
        def _(p):
            kept = known(p)
            values = jnp.concatenate(
                [jnp.where(kept, both_blocks(p, 1), 0.0), jnp.where(kept, 1.0, 0.0)], axis=1
            ).astype(BF16)
            base, lanes = scores_at(p)
            for g in range(group):
                s = decay_a[pl.ds(pl.multiple_of(base + g * tok, tok), tok), lanes]
                highest = jnp.concatenate([top[inner(g), :]] * 2, axis=1)
                w = jnp.exp2((s - highest) * scale).astype(BF16)
                acc[inner(g), :] += jnp.dot(w, values, preferred_element_type=F32)

        for g in range(group):
            attn_out[:, span(g)] = (acc[inner(g), :HEAD_WIDTH] / acc[inner(g), HEAD_WIDTH:]).astype(BF16)

    for head0 in range(0, heads, group):
        attend(head0)

    @pl.when(me > 0)
    def _():
        owners(lambda o, to: p_copy(0, o, me).wait_recv())

    @pl.when(me == 0)
    def _():
        p_in[...] = jnp.zeros_like(p_in)

    entering = p_in[...].reshape(ns * ch, LANES).astype(F32)
    for g in range(ch):
        lanes = slice(g * LANES, (g + 1) * LANES)
        now = entering[g * ns : (g + 1) * ns, :]
        inc_out[0, :, lanes] = now.astype(BF16)
        later = early_fin[:, lanes] + jnp.exp2(rate_s[:, lanes] * sums_a[0:1, lanes]) * now
        inc_out[1, :, lanes] = later.astype(BF16)

    @pl.when(me < n_ctx - 1)
    def _():
        halo.wait_send()
        owners(lambda o, to: e_copy(me, to, o).wait_send())
        owners(lambda o, to: s_copy(o, me, to).wait_send())

    for late in range(2):
        peers(lambda to: part_copy(late, mt, to).wait_send())
    kv_line(lambda to: kv_copy(me, to, kv_send.at[to]).wait_send())

    def end_forward(d):
        src = me - 2 * (d + 1)

        @pl.when(src >= 0)
        def _():
            kv_copy(src, twin, kv_forward.at[src]).wait_send()

    each(steps, end_forward)

    @pl.when(is_owner)
    def _():
        def sent(k):
            @pl.when(k + 1 != me)
            def _():
                p_copy(k + 1, 0, k + 1).wait_send()

        each(n_ctx - 1, sent)


def last_kernel(
    gone, base_y, gate, inc, lhs, attn, mamba_out_hbm, attn_out_hbm, out, attn_sem, out_sem
):
    tok, chans = base_y.shape
    ns = inc.shape[1]
    attn_store = pltpu.make_async_copy(attn, attn_out_hbm, attn_sem)
    attn_store.start()
    stores = []
    for q in range(chans // TILE):
        cols = slice(q * TILE, (q + 1) * TILE)
        for b in range(tok // BLOCK):
            rows = slice(b * BLOCK, (b + 1) * BLOCK)
            held = gone[b * BLOCK * ns : (b + 1) * BLOCK * ns, cols].reshape(BLOCK, ns, TILE)
            held = (held * inc[min(b, 1), :, cols][None]).reshape(BLOCK * ns, TILE)
            y = base_y[rows, cols] + jnp.dot(lhs[rows, :], held, preferred_element_type=F32)
            out[rows, cols] = (y * gate[rows, cols]).astype(BF16)
        stores.append(pltpu.make_async_copy(out.at[:, cols], mamba_out_hbm.at[:, cols], out_sem.at[q]))
        stores[-1].start()
    attn_store.wait()
    for store in stores:
        store.wait()


def shards(
    n_ctx, n_ten,
    length, mamba_in, gate_in, step_raw, conv_weight, conv_bias, step_bias, decay_rates, skip_gain,
    state_proj, query_input_rows, key_input_rows, value_input_rows,
):
    tok, chans = mamba_in.shape
    ch = chans // LANES
    ns = decay_rates.shape[0]
    heads = query_input_rows.shape[1] // HEAD_WIDTH
    group = heads
    while group > 1 and n_ctx * group * tok * LANES > tok * ns * chans:
        group //= 2
    own_lo, n_own = n_ctx // 4, n_ctx // 2
    pieces = ns * ch // n_own
    link = BF16 if pieces % 16 == 0 else F32
    dma = pltpu.SemaphoreType.DMA
    hbm = pl.BlockSpec(memory_space=pl.ANY)
    vmem = pl.BlockSpec(memory_space=pltpu.VMEM)
    ordered = (
        length, mamba_in, step_raw, conv_weight, step_bias.reshape(ch, LANES), decay_rates,
        conv_bias.reshape(ch, LANES), state_proj.T, gate_in, key_input_rows, value_input_rows,
        skip_gain.reshape(ch, LANES), query_input_rows,
    )
    held = [pltpu.SMEM((1,), jnp.int32)]
    held += [pltpu.VMEM(a.shape, a.dtype) for i, a in enumerate(ordered) if i not in (0, 9, 10)]
    channels = pltpu.VMEM((ns, chans), F32)
    halo = ((KW - 1) * ch, LANES)
    parts = pl.pallas_call(
        functools.partial(main_kernel, n_ctx, n_ten, group, own_lo, n_own),
        out_shape=(
            pltpu.VMEM((tok * ns, chans), BF16),
            pltpu.VMEM((tok, chans), F32),
            pltpu.VMEM((tok, chans), F32),
            pltpu.VMEM((2, ns, chans), BF16),
            pltpu.VMEM((tok, BLOCK * ns), BF16),
            pltpu.VMEM(query_input_rows.shape, BF16),
        ),
        in_specs=[hbm] * 13,
        out_specs=(vmem,) * 6,
        scratch_shapes=held + [
            pltpu.VMEM((ch, tok + 8, LANES), F32),
            pltpu.VMEM((tok, chans), BF16),
            pltpu.VMEM((tok, chans), F32),
            pltpu.VMEM((tok, chans), F32),
            channels,
            pltpu.VMEM((ns * ch, LANES), F32),
            pltpu.VMEM((2, chans), F32),
            pltpu.VMEM((tok * ns, LANES), F32),
            pltpu.VMEM((tok * ns, chans), F32),
            pltpu.VMEM((tok * ns, chans), BF16),
            channels,
            channels,
            pltpu.VMEM(halo, F32), pltpu.VMEM(halo, BF16), pltpu.VMEM(halo, BF16),
            pltpu.VMEM((2, n_ten, 2 * ns, tok), F32),
            pltpu.VMEM((n_ctx, ch, LANES), F32),
            pltpu.VMEM((n_own, pieces, LANES), link),
            pltpu.VMEM((n_ctx, pieces, LANES), link),
            pltpu.VMEM((n_ctx, pieces, LANES), link),
            pltpu.VMEM((n_own, pieces, LANES), link),
            pltpu.VMEM((n_ctx, 2, tok, HEAD_WIDTH), BF16),
            pltpu.VMEM((group * tok, tok), F32),
            pltpu.VMEM((group * tok, tok), F32),
            pltpu.VMEM((group * tok, 2 * HEAD_WIDTH), F32),
            dma, dma, dma((2, n_ten)), dma((2, n_ten)),
            dma((n_own,)), dma((n_ctx,)), dma((n_ctx,)), dma((n_own,)),
            dma((n_own,)), dma((n_ctx,)), dma((n_ctx,)), dma((n_ctx,)), dma((n_ctx,)),
            dma((len(ordered),)),
        ],
        compiler_params=pltpu.CompilerParams(
            collective_id=0, has_side_effects=True, vmem_limit_bytes=48 << 20
        ),
    )(*ordered)
    return pl.pallas_call(
        last_kernel,
        out_shape=(
            jax.ShapeDtypeStruct(mamba_in.shape, BF16),
            jax.ShapeDtypeStruct(query_input_rows.shape, BF16),
        ),
        in_specs=[vmem] * 6,
        out_specs=(hbm, hbm),
        scratch_shapes=[pltpu.VMEM((tok, chans), BF16), dma, dma((chans // TILE,))],
        compiler_params=pltpu.CompilerParams(vmem_limit_bytes=16 << 20),
    )(*parts)


def solution(mesh):
    both = P("context", "tensor")
    in_specs = (
        P(), both, both, both, P(None, "tensor"), P("tensor"), P("tensor"), P(None, "tensor"),
        P("tensor"), P("tensor", None), both, both, both,
    )
    body = functools.partial(shards, mesh.shape["context"], mesh.shape["tensor"])
    return jax.shard_map(body, mesh=mesh, in_specs=in_specs, out_specs=(both, both), check_vma=False)
```

```python
import functools
import math

import jax
import jax.numpy as jnp
from jax import lax
from jax.experimental import pallas as pl
from jax.experimental.pallas import tpu as pltpu
from jax.sharding import PartitionSpec as P

KW = 4
HEAD_WIDTH = 128
LANES = 128
BLOCK = 16
WIDE = 512
STEP = 8
TILE = 256
LOG2E = 1.4426950408889634
LOW = -1e30
MESH = pl.DeviceIdType.MESH
F32 = jnp.float32
BF16 = jnp.bfloat16


def each(count, body):
    if count <= 8:
        for i in range(count):
            body(i)
    else:
        @pl.loop(0, count)
        def _(i):
            body(i)


def silu(v):
    return v / (1.0 + jnp.exp(-v))


def block_rows(b, size):
    return pl.ds(pl.multiple_of(b * size, size), size)


def main_kernel(
    n_ctx, n_ten, group, own_lo, n_own,
    length_hbm, mamba_hbm, step_hbm, conv_w_hbm, step_b_hbm, rates_hbm, conv_b_hbm, proj_hbm, gate_hbm,
    keys_hbm, values_hbm, skip_hbm, query_hbm,
    gone_out, base_y, gate_out, inc_out, lhs, attn_out,
    length, mamba, step_raw, conv_w, step_b, rates, conv_b, proj, gate, skip, query,
    x_a, conv_out, step_a, driven, rate_s, rate_flat, sums_a, spread, decay_a, state_a, main_fin, early_fin, early_gone, part_sum,
    halo_f, halo_out, halo_in, part_all, e_all, s_out, s_in, p_out, p_in, kv_all, top, own_scores, acc,
    halo_send, halo_recv, part_send, part_recv, s_send, s_recv, p_send, p_recv, e_send, e_recv,
    kv_send, kv_recv, kv_forward, load_sem,
):
    tok, chans = mamba.shape
    ch = chans // LANES
    ns = rates.shape[0]
    blocks = tok // BLOCK
    pieces = s_out.shape[1]
    me = lax.axis_index("context")
    mt = lax.axis_index("tensor")

    def ctx_copy(src, dst, send, recv, to):
        return pltpu.make_async_remote_copy(
            src_ref=src, dst_ref=dst, send_sem=send, recv_sem=recv,
            device_id={"context": to}, device_id_type=MESH,
        )

    sources = (
        mamba_hbm, step_hbm, length_hbm, conv_w_hbm, step_b_hbm, rates_hbm, conv_b_hbm, proj_hbm, gate_hbm,
        keys_hbm, values_hbm, skip_hbm, query_hbm,
    )
    targets = (
        mamba, step_raw, length, conv_w, step_b, rates, conv_b, proj, gate,
        kv_all.at[me, 0], kv_all.at[me, 1], skip, query,
    )
    loads = [
        pltpu.make_async_copy(src, dst, load_sem.at[i])
        for i, (src, dst) in enumerate(zip(sources, targets))
    ]
    for load in loads[:2]:
        load.start()

    barrier = pltpu.get_barrier_semaphore()
    for d in range(1, n_ten):
        pl.semaphore_signal(
            barrier, inc=1, device_id={"tensor": lax.rem(mt + d, n_ten)}, device_id_type=MESH
        )

    def owns(k):
        return jnp.logical_and(k >= own_lo, k < own_lo + n_own)

    is_owner = owns(me)

    def meets(k):
        near = jnp.logical_or(lax.rem(k - me + n_ctx, 2) == 0, jnp.abs(k - me) == 1)
        return jnp.logical_or(jnp.logical_or(owns(k), is_owner), near)

    def greet(to):
        @pl.when(meets(to))
        def _():
            pl.semaphore_signal(barrier, inc=1, device_id={"context": to}, device_id_type=MESH)

    each(n_ctx - 1, lambda d: greet(lax.rem(me + d + 1, n_ctx)))

    def count_met(d, total):
        return total + jnp.where(meets(lax.rem(me + d + 1, n_ctx)), 1, 0)

    met = jnp.int32(n_ten - 1)
    if n_ctx <= 8:
        for d in range(n_ctx - 1):
            met = count_met(d, met)
    else:
        met = lax.fori_loop(0, n_ctx - 1, count_met, met)

    for load in loads[2:]:
        load.start()

    first = me * tok
    for load in loads[:7]:
        load.wait()
    prompt_end = length[0]
    valid = (first + lax.broadcasted_iota(jnp.int32, (tok, LANES), 0)) < prompt_end
    conv_out[0:BLOCK, :] = jnp.zeros((BLOCK, chans), BF16)

    def convolve(g, lanes, start, count):
        total = jnp.broadcast_to(conv_b[pl.ds(g, 1), :], (count, LANES))
        for j in range(KW):
            at = 8 + start - (KW - 1) + j
            total = total + conv_w[j : j + 1, lanes] * x_a[g, at : at + count, :]
        mixed = silu(total).astype(BF16)
        conv_out[start : start + count, lanes] = mixed
        driven[start : start + count, lanes] = step_a[start : start + count, lanes] * mixed.astype(F32)

    @pl.loop(0, ch)
    def _(g):
        lanes = block_rows(g, LANES)
        x = mamba[:, lanes].astype(F32)
        x_a[g, 8 : 8 + tok, :] = x
        for j in range(KW - 1):
            at = tok - (KW - 1) + j
            halo_f[pl.ds(j * ch + g, 1), :] = x[at : at + 1, :]
        raw = step_raw[:, lanes].astype(F32) + step_b[pl.ds(g, 1), :]
        size = jnp.maximum(raw, 0.0) + jnp.log(1.0 + jnp.exp(-jnp.abs(raw)))
        size = jnp.where(valid, size, 0.0)
        step_a[:, lanes] = size
        early = jnp.sum(size[:BLOCK], axis=0, keepdims=True)
        late = jnp.sum(size[BLOCK:], axis=0, keepdims=True)
        sums_a[0:1, lanes] = early
        sums_a[1:2, lanes] = late
        e_all[me, pl.ds(g, 1), :] = early + late
        scaled = rates[:, lanes] * (-LOG2E)
        rate_s[:, lanes] = scaled
        rate_flat[block_rows(g, ns), :] = scaled
        convolve(g, lanes, BLOCK, tok - BLOCK)

    halo_out[...] = halo_f[...].astype(BF16)
    loads[7].wait()

    def partial_projection(count):
        return lax.dot_general(
            proj[...], conv_out[0:count, :], (((1,), (1,)), ((), ())), preferred_element_type=F32
        )

    part_all[0, mt] = partial_projection(tok)

    for load in loads[8:]:
        load.wait()

    pl.semaphore_wait(barrier, met)

    halo = ctx_copy(halo_out, halo_in, halo_send, halo_recv, lax.rem(me + 1, n_ctx))

    @pl.when(me < n_ctx - 1)
    def _():
        halo.start()

    def part_copy(late, src, to):
        return pltpu.make_async_remote_copy(
            src_ref=part_all.at[late, src], dst_ref=part_all.at[late, src],
            send_sem=part_send.at[late, to], recv_sem=part_recv.at[late, src],
            device_id={"tensor": to}, device_id_type=MESH,
        )

    def peers(body):
        for d in range(1, n_ten):
            body(lax.rem(mt + d, n_ten))

    peers(lambda to: part_copy(0, mt, to).start())

    def owners(body):
        def visit(o):
            to = own_lo + o

            @pl.when(to != me)
            def _():
                body(o, to)

        each(n_own, visit)

    def e_copy(src, to, slot):
        return ctx_copy(e_all.at[src], e_all.at[src], e_send.at[slot], e_recv.at[src], to)

    @pl.when(me < n_ctx - 1)
    def _():
        owners(lambda o, to: e_copy(me, to, o).start())

    twin = me + 1 - 2 * lax.rem(me, 2)
    steps = n_ctx // 2 - 1

    def kv_copy(src, to, send):
        return ctx_copy(kv_all.at[src], kv_all.at[src], send, kv_recv.at[src], to)

    def kv_line(body):
        def visit(d):
            to = me + 2 * (d + 1)

            @pl.when(to < n_ctx)
            def _():
                body(to)

        each(n_ctx // 2 - 1, visit)

        @pl.when(lax.rem(me, 2) == 0)
        def _():
            body(me + 1)

    kv_line(lambda to: kv_copy(me, to, kv_send.at[to]).start())

    def forward(d):
        src = me - 2 * (d + 1)

        @pl.when(src >= 0)
        def _():
            kv_copy(src, twin, kv_forward.at[src]).wait_recv()
            kv_copy(src, twin, kv_forward.at[src]).start()

    chunks = [slice(q * WIDE, (q + 1) * WIDE) for q in range(chans // WIDE)]

    def decays(i):
        t0 = pl.multiple_of(i * STEP, STEP)
        for q in range(chans // TILE):
            cols = slice(q * TILE, (q + 1) * TILE)
            rate = rate_s[:, cols]
            for k in range(STEP):
                size = jnp.broadcast_to(step_a[pl.ds(t0 + k, 1), cols], (ns, TILE))
                decay_a[block_rows(t0 + k, ns), cols] = jnp.exp2(rate * size)

    pl.loop(0, tok // STEP * 7 // 8)(decays)

    @pl.when(me > 0)
    def _():
        halo.wait_recv()
        halo_f[...] = halo_in[...].astype(F32)

    @pl.when(me == 0)
    def _():
        halo_f[...] = jnp.zeros_like(halo_f)

    @pl.loop(0, ch)
    def _(g):
        for j in range(KW - 1):
            at = 8 - (KW - 1) + j
            x_a[g, at : at + 1, :] = halo_f[pl.ds(j * ch + g, 1), :]
        convolve(g, block_rows(g, LANES), 0, BLOCK)

    part_all[1, mt] = jnp.concatenate(
        [partial_projection(BLOCK), jnp.zeros((2 * ns, tok - BLOCK), F32)], axis=1
    )
    peers(lambda to: part_copy(1, mt, to).start())
    pl.loop(tok // STEP * 7 // 8, tok // STEP)(decays)

    def collect(late, start, stop):
        peers(lambda src: part_copy(late, src, mt).wait_recv())
        projected = part_all[late, 0]
        for d in range(1, n_ten):
            projected = projected + part_all[late, d]
        for t in range(start, stop):
            spread[t * ns : (t + 1) * ns, :] = jnp.broadcast_to(projected[:ns, t : t + 1], (ns, LANES))
        part_sum[late] = projected[ns:]

    def spread_readout():
        early = lax.broadcasted_iota(jnp.int32, (ns, tok), 1) < BLOCK
        readout = jnp.where(early, part_sum[1], part_sum[0])
        source = lax.broadcasted_iota(jnp.int32, (ns, BLOCK * ns), 0)
        entry = lax.rem(lax.broadcasted_iota(jnp.int32, (ns, BLOCK * ns), 1), ns)
        pick = jnp.where(source == entry, 1.0, 0.0).astype(BF16)
        wide = jnp.dot(readout.T.astype(BF16), pick, preferred_element_type=F32)
        token = lax.rem(lax.broadcasted_iota(jnp.int32, wide.shape, 0), BLOCK)
        owner = lax.broadcasted_iota(jnp.int32, wide.shape, 1) // ns
        lhs[...] = jnp.where(token == owner, wide, 0.0).astype(BF16)

    collect(0, BLOCK, tok)

    def advance(i, state, cols):
        t0 = pl.multiple_of(i * STEP, STEP)
        for k in range(STEP):
            rows = block_rows(t0 + k, ns)
            inject = jnp.concatenate([spread[rows, :]] * (WIDE // LANES), axis=1)
            drive = inject * jnp.broadcast_to(driven[pl.ds(t0 + k, 1), cols], (ns, WIDE))
            state = decay_a[rows, cols] * state + drive
            state_a[rows, cols] = state.astype(BF16)
        return state

    still = jnp.zeros((ns, WIDE), F32)
    for cols in chunks:
        main_fin[:, cols] = lax.fori_loop(
            BLOCK // STEP, tok // STEP, lambda i, state: advance(i, state, cols), still
        )

    collect(1, 0, BLOCK)
    forward(0)

    def s_copy(o, src, to):
        return ctx_copy(s_out.at[o], s_in.at[src], s_send.at[o], s_recv.at[src], to)

    share = n_own // len(chunks)
    for q, cols in enumerate(chunks):
        early = still
        for i in range(BLOCK // STEP):
            early = advance(i, early, cols)
        early_fin[:, cols] = early
        early_gone[:, cols] = jnp.exp2(rate_s[:, cols] * sums_a[0:1, cols])
        final = main_fin[:, cols] + jnp.exp2(rate_s[:, cols] * sums_a[1:2, cols]) * early
        flat = jnp.concatenate([final[:, k * LANES : (k + 1) * LANES] for k in range(WIDE // LANES)], axis=0)
        s_out[q * share : (q + 1) * share] = flat.astype(s_out.dtype).reshape(share, pieces, LANES)

        def send(i):
            o = q * share + i
            to = own_lo + o

            @pl.when(jnp.logical_and(to != me, me < n_ctx - 1))
            def _():
                s_copy(o, me, to).start()

        each(share, send)

    each(steps - 1, lambda d: forward(d + 1))
    spread_readout()

    @pl.loop(0, ch)
    def _(g):
        lanes = block_rows(g, LANES)
        gate_out[:, lanes] = silu(gate[:, lanes].astype(F32))

    for cols in chunks:
        def shrink(i, gone):
            t0 = pl.multiple_of(i * STEP, STEP)
            for k in range(STEP):
                rows = block_rows(t0 + k, ns)
                gone = gone * decay_a[rows, cols]
                gone_out[rows, cols] = gone.astype(BF16)
            return gone

        whole = jnp.ones((ns, WIDE), F32)
        lax.fori_loop(0, BLOCK // STEP, shrink, whole)
        lax.fori_loop(BLOCK // STEP, tok // STEP, shrink, whole)

    @pl.loop(0, blocks)
    def _(b):
        rows = block_rows(b, BLOCK)
        left = lhs[rows, :]
        for q in range(chans // TILE):
            cols = slice(q * TILE, (q + 1) * TILE)
            gain = jnp.concatenate(
                [skip[g : g + 1, :] for g in range(q * TILE // LANES, (q + 1) * TILE // LANES)], axis=1
            )
            base_y[rows, cols] = gain * conv_out[rows, cols].astype(F32) + jnp.dot(
                left, state_a[block_rows(b, BLOCK * ns), cols], preferred_element_type=F32
            )

    def p_copy(k, o, to):
        return ctx_copy(p_out.at[k], p_in.at[o], p_send.at[k], p_recv.at[o], to)

    @pl.when(is_owner)
    def _():
        o = me - own_lo
        s_in[me] = s_out[o]
        my_rate = rate_flat[pl.ds(o * pieces, pieces), :]

        def send(k):
            @pl.when(k != me)
            def _():
                p_copy(k, o, k).start()

        def fold(j, running):
            @pl.when(j != me)
            def _():
                e_copy(j, me, 0).wait_recv()
                s_copy(0, j, me).wait_recv()

            if pieces >= ns:
                count = pieces // ns
                gone = jnp.concatenate(
                    [
                        jnp.broadcast_to(e_all[j, pl.ds(o * count + i, 1), :], (ns, LANES))
                        for i in range(count)
                    ],
                    axis=0,
                )
            else:
                gone = jnp.broadcast_to(e_all[j, pl.ds(o * pieces // ns, 1), :], (pieces, LANES))
            running = jnp.exp2(my_rate * gone) * running + s_in[j].astype(F32)
            p_out[j + 1] = running.astype(p_out.dtype)
            send(j + 1)
            return running

        running = jnp.zeros((pieces, LANES), F32)
        if n_ctx <= 8:
            for j in range(n_ctx - 1):
                running = fold(j, running)
        else:
            running = lax.fori_loop(0, n_ctx - 1, fold, running)

        p_in[o] = p_out[me]

    scale = LOG2E / math.sqrt(HEAD_WIDTH)
    heads = query.shape[1] // HEAD_WIDTH
    high = group * tok
    bands = decay_a.shape[0] // high
    side = lax.rem(me, 2)
    key_end = jnp.minimum(prompt_end, first)
    diagonal_iota = lax.broadcasted_iota(jnp.int32, (tok, tok), 1)
    allowed = jnp.logical_and(
        diagonal_iota <= lax.broadcasted_iota(jnp.int32, (tok, tok), 0), diagonal_iota + first < prompt_end
    )

    def inner(g):
        return slice(g * tok, (g + 1) * tok)

    def scores_at(p, g):
        base = pl.multiple_of(lax.rem(p, bands) * high + g * tok, tok)
        return pl.ds(base, tok), block_rows(p // bands, 2 * tok)

    def dot_keys(q, keys):
        return lax.dot_general(q, keys, (((1,), (1,)), ((), ())), preferred_element_type=F32)

    def known(p, parity):
        at = lax.broadcasted_iota(jnp.int32, (2 * tok, HEAD_WIDTH), 0)
        return at + jnp.where(at >= tok, tok, 0) + (parity + 4 * p) * tok < key_end

    def both_blocks(p, parity, what):
        one = parity + 4 * p
        two = jnp.minimum(one + 2, me)
        return jnp.concatenate([kv_all[one, what], kv_all[two, what]], axis=0).astype(F32)

    def score(head0, parity, pairs, highest):
        @pl.loop(0, pairs)
        def _(p):
            stand_in = jnp.broadcast_to(kv_all[parity, 0, 0:1, :].astype(F32), (2 * tok, HEAD_WIDTH))
            keys = jnp.where(known(p, parity), both_blocks(p, parity, 0), stand_in).astype(BF16)
            for g in range(group):
                s = dot_keys(query[:, span(head0, g)], keys)
                rows, lanes = scores_at(p, g)
                decay_a[rows, lanes] = s
                highest[inner(g), :] = jnp.maximum(highest[inner(g), :], jnp.maximum(s[:, :tok], s[:, tok:]))

    def gather(parity, pairs):
        @pl.loop(0, pairs)
        def _(p):
            kept = known(p, parity)
            values = jnp.concatenate(
                [jnp.where(kept, both_blocks(p, parity, 1), 0.0), jnp.where(kept, 1.0, 0.0)], axis=1
            ).astype(BF16)
            for g in range(group):
                rows, lanes = scores_at(p, g)
                highest = jnp.concatenate([top[inner(g), :]] * 2, axis=1)
                w = jnp.exp2((decay_a[rows, lanes] - highest) * scale).astype(BF16)
                acc[inner(g), :] += jnp.dot(w, values, preferred_element_type=F32)

    def span(head0, g):
        return slice((head0 + g) * HEAD_WIDTH, (head0 + g + 1) * HEAD_WIDTH)

    def row_max(ref, g):
        return jnp.broadcast_to(jnp.max(ref[inner(g), :], axis=1, keepdims=True), (tok, tok))

    near_pairs = (me // 2 + 1) // 2
    far_pairs = ((me + 1) // 2 + 1) // 2

    def attend_near(head0):
        own_keys = kv_all[me, 0]
        for g in range(group):
            s = jnp.where(allowed, dot_keys(query[:, span(head0, g)], own_keys), LOW)
            own_scores[inner(g), :] = s
            top[inner(g), :] = s
        score(head0, side, near_pairs, top)
        own_values = jnp.concatenate([kv_all[me, 1], jnp.ones((tok, HEAD_WIDTH), BF16)], axis=1)
        for g in range(group):
            highest = row_max(top, g)
            top[inner(g), :] = highest
            w = jnp.exp2((own_scores[inner(g), :] - highest) * scale).astype(BF16)
            acc[inner(g), :] = jnp.dot(w, own_values, preferred_element_type=F32)
        gather(side, near_pairs)

    def attend_far(head0):
        own_scores[...] = top[...]
        score(head0, 1 - side, far_pairs, own_scores)
        for g in range(group):
            highest = row_max(own_scores, g)
            shrunk = jnp.exp2((top[inner(g), :] - highest) * scale)
            acc[inner(g), :] = acc[inner(g), :] * jnp.concatenate([shrunk] * 2, axis=1)
            top[inner(g), :] = highest
        gather(1 - side, far_pairs)
        for g in range(group):
            attn_out[:, span(head0, g)] = (acc[inner(g), :HEAD_WIDTH] / acc[inner(g), HEAD_WIDTH:]).astype(BF16)

    attend_near(0)

    def arrive(d):
        src = twin - 2 * (d + 1)

        @pl.when(src >= 0)
        def _():
            kv_copy(src, twin, kv_send.at[src]).wait_recv()

    each(steps, arrive)

    @pl.when(lax.rem(me, 2) == 1)
    def _():
        kv_copy(me - 1, twin, kv_send.at[0]).wait_recv()

    attend_far(0)
    for head0 in range(group, heads, group):
        attend_near(head0)
        attend_far(head0)

    @pl.when(me < n_ctx - 1)
    def _():
        halo.wait_send()
        owners(lambda o, to: e_copy(me, to, o).wait_send())
        owners(lambda o, to: s_copy(o, me, to).wait_send())

    for late in range(2):
        peers(lambda to: part_copy(late, mt, to).wait_send())
    kv_line(lambda to: kv_copy(me, to, kv_send.at[to]).wait_send())

    def end_forward(d):
        src = me - 2 * (d + 1)

        @pl.when(src >= 0)
        def _():
            kv_copy(src, twin, kv_forward.at[src]).wait_send()

    each(steps, end_forward)

    @pl.when(is_owner)
    def _():
        def sent(k):
            @pl.when(k + 1 != me)
            def _():
                p_copy(k + 1, 0, k + 1).wait_send()

        each(n_ctx - 1, sent)

    @pl.when(me > 0)
    def _():
        owners(lambda o, to: p_copy(0, o, me).wait_recv())

    @pl.when(me == 0)
    def _():
        p_in[...] = jnp.zeros_like(p_in)

    entering = p_in[...].reshape(ns * ch, LANES).astype(F32)
    for g in range(ch):
        lanes = slice(g * LANES, (g + 1) * LANES)
        now = entering[g * ns : (g + 1) * ns, :]
        inc_out[0, :, lanes] = now.astype(BF16)
        inc_out[1, :, lanes] = (early_fin[:, lanes] + early_gone[:, lanes] * now).astype(BF16)


def last_kernel(
    gone, base_y, gate, inc, lhs, attn, mamba_out_hbm, attn_out_hbm, out, attn_sem, out_sem
):
    tok, chans = base_y.shape
    ns = inc.shape[1]
    attn_store = pltpu.make_async_copy(attn, attn_out_hbm, attn_sem)
    attn_store.start()
    stores = []
    for q in range(chans // TILE):
        cols = slice(q * TILE, (q + 1) * TILE)
        for b in range(tok // BLOCK):
            rows = slice(b * BLOCK, (b + 1) * BLOCK)
            held = gone[b * BLOCK * ns : (b + 1) * BLOCK * ns, cols].reshape(BLOCK, ns, TILE)
            held = (held * inc[min(b, 1), :, cols][None]).reshape(BLOCK * ns, TILE)
            y = base_y[rows, cols] + jnp.dot(lhs[rows, :], held, preferred_element_type=F32)
            out[rows, cols] = (y * gate[rows, cols]).astype(BF16)
        stores.append(pltpu.make_async_copy(out.at[:, cols], mamba_out_hbm.at[:, cols], out_sem.at[q]))
        stores[-1].start()
    attn_store.wait()
    for store in stores:
        store.wait()


def shards(
    n_ctx, n_ten,
    length, mamba_in, gate_in, step_raw, conv_weight, conv_bias, step_bias, decay_rates, skip_gain,
    state_proj, query_input_rows, key_input_rows, value_input_rows,
):
    tok, chans = mamba_in.shape
    ch = chans // LANES
    ns = decay_rates.shape[0]
    heads = query_input_rows.shape[1] // HEAD_WIDTH
    group = heads
    while group > 1 and n_ctx * group * tok * LANES > tok * ns * chans:
        group //= 2
    own_lo, n_own = n_ctx // 4, n_ctx // 2
    pieces = ns * ch // n_own
    link = BF16 if pieces % 16 == 0 else F32
    dma = pltpu.SemaphoreType.DMA
    hbm = pl.BlockSpec(memory_space=pl.ANY)
    vmem = pl.BlockSpec(memory_space=pltpu.VMEM)
    ordered = (
        length, mamba_in, step_raw, conv_weight, step_bias.reshape(ch, LANES), decay_rates,
        conv_bias.reshape(ch, LANES), state_proj.T, gate_in, key_input_rows, value_input_rows,
        skip_gain.reshape(ch, LANES), query_input_rows,
    )
    held = [pltpu.SMEM((1,), jnp.int32)]
    held += [pltpu.VMEM(a.shape, a.dtype) for i, a in enumerate(ordered) if i not in (0, 9, 10)]
    channels = pltpu.VMEM((ns, chans), F32)
    halo = ((KW - 1) * ch, LANES)
    parts = pl.pallas_call(
        functools.partial(main_kernel, n_ctx, n_ten, group, own_lo, n_own),
        out_shape=(
            pltpu.VMEM((tok * ns, chans), BF16),
            pltpu.VMEM((tok, chans), F32),
            pltpu.VMEM((tok, chans), F32),
            pltpu.VMEM((2, ns, chans), BF16),
            pltpu.VMEM((tok, BLOCK * ns), BF16),
            pltpu.VMEM(query_input_rows.shape, BF16),
        ),
        in_specs=[hbm] * 13,
        out_specs=(vmem,) * 6,
        scratch_shapes=held + [
            pltpu.VMEM((ch, tok + 8, LANES), F32),
            pltpu.VMEM((tok, chans), BF16),
            pltpu.VMEM((tok, chans), F32),
            pltpu.VMEM((tok, chans), F32),
            channels,
            pltpu.VMEM((ns * ch, LANES), F32),
            pltpu.VMEM((2, chans), F32),
            pltpu.VMEM((tok * ns, LANES), F32),
            pltpu.VMEM((tok * ns, chans), F32),
            pltpu.VMEM((tok * ns, chans), BF16),
            channels,
            channels,
            channels,
            pltpu.VMEM((2, ns, tok), F32),
            pltpu.VMEM(halo, F32), pltpu.VMEM(halo, BF16), pltpu.VMEM(halo, BF16),
            pltpu.VMEM((2, n_ten, 2 * ns, tok), F32),
            pltpu.VMEM((n_ctx, ch, LANES), F32),
            pltpu.VMEM((n_own, pieces, LANES), link),
            pltpu.VMEM((n_ctx, pieces, LANES), link),
            pltpu.VMEM((n_ctx, pieces, LANES), link),
            pltpu.VMEM((n_own, pieces, LANES), link),
            pltpu.VMEM((n_ctx, 2, tok, HEAD_WIDTH), BF16),
            pltpu.VMEM((group * tok, tok), F32),
            pltpu.VMEM((group * tok, tok), F32),
            pltpu.VMEM((group * tok, 2 * HEAD_WIDTH), F32),
            dma, dma, dma((2, n_ten)), dma((2, n_ten)),
            dma((n_own,)), dma((n_ctx,)), dma((n_ctx,)), dma((n_own,)),
            dma((n_own,)), dma((n_ctx,)), dma((n_ctx,)), dma((n_ctx,)), dma((n_ctx,)),
            dma((len(ordered),)),
        ],
        compiler_params=pltpu.CompilerParams(
            collective_id=0, has_side_effects=True, vmem_limit_bytes=48 << 20
        ),
    )(*ordered)
    return pl.pallas_call(
        last_kernel,
        out_shape=(
            jax.ShapeDtypeStruct(mamba_in.shape, BF16),
            jax.ShapeDtypeStruct(query_input_rows.shape, BF16),
        ),
        in_specs=[vmem] * 6,
        out_specs=(hbm, hbm),
        scratch_shapes=[pltpu.VMEM((tok, chans), BF16), dma, dma((chans // TILE,))],
        compiler_params=pltpu.CompilerParams(vmem_limit_bytes=16 << 20),
    )(*parts)


def solution(mesh):
    both = P("context", "tensor")
    in_specs = (
        P(), both, both, both, P(None, "tensor"), P("tensor"), P("tensor"), P(None, "tensor"),
        P("tensor"), P("tensor", None), both, both, both,
    )
    body = functools.partial(shards, mesh.shape["context"], mesh.shape["tensor"])
    return jax.shard_map(body, mesh=mesh, in_specs=in_specs, out_specs=(both, both), check_vma=False)
```

```python
import functools
import math

import jax
import jax.numpy as jnp
from jax import lax
from jax.experimental import pallas as pl
from jax.experimental.pallas import tpu as pltpu
from jax.sharding import PartitionSpec as P

KW = 4
HEAD_WIDTH = 128
LANES = 128
BLOCK = 16
WIDE = 512
STEP = 8
TILE = 256
LOG2E = 1.4426950408889634
LOW = -1e30
MESH = pl.DeviceIdType.MESH
F32 = jnp.float32
BF16 = jnp.bfloat16


def each(count, body):
    if count <= 8:
        for i in range(count):
            body(i)
    else:
        @pl.loop(0, count)
        def _(i):
            body(i)


def silu(v):
    return v / (1.0 + jnp.exp(-v))


def block_rows(b, size):
    return pl.ds(pl.multiple_of(b * size, size), size)


def main_kernel(
    n_ctx, n_ten, group, own_lo, n_own,
    length_hbm, mamba_hbm, step_hbm, conv_w_hbm, step_b_hbm, rates_hbm, conv_b_hbm, proj_hbm, gate_hbm,
    keys_hbm, values_hbm, skip_hbm, query_hbm,
    gone_out, base_y, gate_out, inc_out, lhs, attn_out,
    length, mamba, step_raw, conv_w, step_b, rates, conv_b, proj, gate, skip, query,
    x_a, conv_out, step_a, driven, rate_s, rate_flat, sums_a, spread, decay_a, state_a, main_fin, early_fin, early_gone, part_sum, block_gone,
    halo_f, halo_out, halo_in, part_all, e_all, s_out, s_in, p_out, p_in, kv_all, top, own_scores, acc,
    halo_send, halo_recv, part_send, part_recv, s_send, s_recv, p_send, p_recv, e_send, e_recv,
    kv_send, kv_recv, kv_forward, load_sem,
):
    tok, chans = mamba.shape
    ch = chans // LANES
    ns = rates.shape[0]
    blocks = tok // BLOCK
    pieces = s_out.shape[1]
    me = lax.axis_index("context")
    mt = lax.axis_index("tensor")

    def ctx_copy(src, dst, send, recv, to):
        return pltpu.make_async_remote_copy(
            src_ref=src, dst_ref=dst, send_sem=send, recv_sem=recv,
            device_id={"context": to}, device_id_type=MESH,
        )

    sources = (
        mamba_hbm, step_hbm, length_hbm, conv_w_hbm, step_b_hbm, rates_hbm, conv_b_hbm, proj_hbm, gate_hbm,
        keys_hbm, values_hbm, skip_hbm, query_hbm,
    )
    targets = (
        mamba, step_raw, length, conv_w, step_b, rates, conv_b, proj, gate,
        kv_all.at[me, 0], kv_all.at[me, 1], skip, query,
    )
    loads = [
        pltpu.make_async_copy(src, dst, load_sem.at[i])
        for i, (src, dst) in enumerate(zip(sources, targets))
    ]
    for load in loads[:2]:
        load.start()

    barrier = pltpu.get_barrier_semaphore()
    for d in range(1, n_ten):
        pl.semaphore_signal(
            barrier, inc=1, device_id={"tensor": lax.rem(mt + d, n_ten)}, device_id_type=MESH
        )

    def owns(k):
        return jnp.logical_and(k >= own_lo, k < own_lo + n_own)

    is_owner = owns(me)

    def meets(k):
        near = jnp.logical_or(lax.rem(k - me + n_ctx, 2) == 0, jnp.abs(k - me) == 1)
        return jnp.logical_or(jnp.logical_or(owns(k), is_owner), near)

    def greet(to):
        @pl.when(meets(to))
        def _():
            pl.semaphore_signal(barrier, inc=1, device_id={"context": to}, device_id_type=MESH)

    each(n_ctx - 1, lambda d: greet(lax.rem(me + d + 1, n_ctx)))

    def count_met(d, total):
        return total + jnp.where(meets(lax.rem(me + d + 1, n_ctx)), 1, 0)

    met = jnp.int32(n_ten - 1)
    if n_ctx <= 8:
        for d in range(n_ctx - 1):
            met = count_met(d, met)
    else:
        met = lax.fori_loop(0, n_ctx - 1, count_met, met)

    for load in loads[2:]:
        load.start()

    first = me * tok
    for load in loads[:7]:
        load.wait()
    prompt_end = length[0]
    valid = (first + lax.broadcasted_iota(jnp.int32, (tok, LANES), 0)) < prompt_end
    conv_out[0:BLOCK, :] = jnp.zeros((BLOCK, chans), BF16)

    def convolve(g, lanes, start, count):
        total = jnp.broadcast_to(conv_b[pl.ds(g, 1), :], (count, LANES))
        for j in range(KW):
            at = 8 + start - (KW - 1) + j
            total = total + conv_w[j : j + 1, lanes] * x_a[g, at : at + count, :]
        mixed = silu(total).astype(BF16)
        conv_out[start : start + count, lanes] = mixed
        driven[start : start + count, lanes] = step_a[start : start + count, lanes] * mixed.astype(F32)

    @pl.loop(0, ch)
    def _(g):
        lanes = block_rows(g, LANES)
        x = mamba[:, lanes].astype(F32)
        x_a[g, 8 : 8 + tok, :] = x
        for j in range(KW - 1):
            at = tok - (KW - 1) + j
            halo_f[pl.ds(j * ch + g, 1), :] = x[at : at + 1, :]
        raw = step_raw[:, lanes].astype(F32) + step_b[pl.ds(g, 1), :]
        size = jnp.maximum(raw, 0.0) + jnp.log(1.0 + jnp.exp(-jnp.abs(raw)))
        size = jnp.where(valid, size, 0.0)
        step_a[:, lanes] = size
        early = jnp.sum(size[:BLOCK], axis=0, keepdims=True)
        late = jnp.sum(size[BLOCK:], axis=0, keepdims=True)
        sums_a[0:1, lanes] = early
        sums_a[1:2, lanes] = late
        e_all[me, pl.ds(g, 1), :] = early + late
        scaled = rates[:, lanes] * (-LOG2E)
        rate_s[:, lanes] = scaled
        rate_flat[block_rows(g, ns), :] = scaled
        convolve(g, lanes, BLOCK, tok - BLOCK)

    halo_out[...] = halo_f[...].astype(BF16)
    loads[7].wait()

    def partial_projection(count):
        return lax.dot_general(
            proj[...], conv_out[0:count, :], (((1,), (1,)), ((), ())), preferred_element_type=F32
        )

    part_all[0, mt] = partial_projection(tok)

    for load in loads[8:]:
        load.wait()

    pl.semaphore_wait(barrier, met)

    halo = ctx_copy(halo_out, halo_in, halo_send, halo_recv, lax.rem(me + 1, n_ctx))

    @pl.when(me < n_ctx - 1)
    def _():
        halo.start()

    def part_copy(late, src, to):
        return pltpu.make_async_remote_copy(
            src_ref=part_all.at[late, src], dst_ref=part_all.at[late, src],
            send_sem=part_send.at[late, to], recv_sem=part_recv.at[late, src],
            device_id={"tensor": to}, device_id_type=MESH,
        )

    def peers(body):
        for d in range(1, n_ten):
            body(lax.rem(mt + d, n_ten))

    peers(lambda to: part_copy(0, mt, to).start())

    def owners(body):
        def visit(o):
            to = own_lo + o

            @pl.when(to != me)
            def _():
                body(o, to)

        each(n_own, visit)

    def e_copy(src, to, slot):
        return ctx_copy(e_all.at[src], e_all.at[src], e_send.at[slot], e_recv.at[src], to)

    @pl.when(me < n_ctx - 1)
    def _():
        owners(lambda o, to: e_copy(me, to, o).start())

    twin = me + 1 - 2 * lax.rem(me, 2)
    steps = n_ctx // 2 - 1

    def kv_copy(src, to, send):
        return ctx_copy(kv_all.at[src], kv_all.at[src], send, kv_recv.at[src], to)

    def kv_line(body):
        def visit(d):
            to = me + 2 * (d + 1)

            @pl.when(to < n_ctx)
            def _():
                body(to)

        each(n_ctx // 2 - 1, visit)

        @pl.when(lax.rem(me, 2) == 0)
        def _():
            body(me + 1)

    kv_line(lambda to: kv_copy(me, to, kv_send.at[to]).start())

    def forward(d):
        src = me - 2 * (d + 1)

        @pl.when(src >= 0)
        def _():
            kv_copy(src, twin, kv_forward.at[src]).wait_recv()
            kv_copy(src, twin, kv_forward.at[src]).start()

    chunks = [slice(q * WIDE, (q + 1) * WIDE) for q in range(chans // WIDE)]

    def decays(i):
        t0 = pl.multiple_of(i * STEP, STEP)
        for q in range(chans // TILE):
            cols = slice(q * TILE, (q + 1) * TILE)
            rate = rate_s[:, cols]
            for k in range(STEP):
                size = jnp.broadcast_to(step_a[pl.ds(t0 + k, 1), cols], (ns, TILE))
                decay_a[block_rows(t0 + k, ns), cols] = jnp.exp2(rate * size)

    pl.loop(0, tok // STEP * 7 // 8)(decays)

    @pl.when(me > 0)
    def _():
        halo.wait_recv()
        halo_f[...] = halo_in[...].astype(F32)

    @pl.when(me == 0)
    def _():
        halo_f[...] = jnp.zeros_like(halo_f)

    @pl.loop(0, ch // 4)
    def _(i):
        for g in [i * 4 + k for k in range(4)]:
            for j in range(KW - 1):
                at = 8 - (KW - 1) + j
                x_a[g, at : at + 1, :] = halo_f[pl.ds(j * ch + g, 1), :]
        for g in [i * 4 + k for k in range(4)]:
            convolve(g, block_rows(g, LANES), 0, BLOCK)

    part_all[1, mt] = jnp.concatenate(
        [partial_projection(BLOCK), jnp.zeros((2 * ns, tok - BLOCK), F32)], axis=1
    )
    peers(lambda to: part_copy(1, mt, to).start())
    pl.loop(tok // STEP * 7 // 8, tok // STEP)(decays)

    def collect(late, start, stop):
        peers(lambda src: part_copy(late, src, mt).wait_recv())
        projected = part_all[late, 0]
        for d in range(1, n_ten):
            projected = projected + part_all[late, d]
        for t in range(start, stop):
            spread[t * ns : (t + 1) * ns, :] = jnp.broadcast_to(projected[:ns, t : t + 1], (ns, LANES))
        part_sum[late] = projected[ns:]

    def spread_readout():
        early = lax.broadcasted_iota(jnp.int32, (ns, tok), 1) < BLOCK
        readout = jnp.where(early, part_sum[1], part_sum[0])
        source = lax.broadcasted_iota(jnp.int32, (ns, BLOCK * ns), 0)
        entry = lax.rem(lax.broadcasted_iota(jnp.int32, (ns, BLOCK * ns), 1), ns)
        pick = jnp.where(source == entry, 1.0, 0.0).astype(BF16)
        wide = jnp.dot(readout.T.astype(BF16), pick, preferred_element_type=F32)
        token = lax.rem(lax.broadcasted_iota(jnp.int32, wide.shape, 0), BLOCK)
        owner = lax.broadcasted_iota(jnp.int32, wide.shape, 1) // ns
        lhs[...] = jnp.where(token == owner, wide, 0.0).astype(BF16)

    collect(0, BLOCK, tok)

    def advance(i, state, cols):
        t0 = pl.multiple_of(i * STEP, STEP)
        for k in range(STEP):
            rows = block_rows(t0 + k, ns)
            inject = jnp.concatenate([spread[rows, :]] * (WIDE // LANES), axis=1)
            drive = inject * jnp.broadcast_to(driven[pl.ds(t0 + k, 1), cols], (ns, WIDE))
            state = decay_a[rows, cols] * state + drive
            state_a[rows, cols] = state.astype(BF16)
        return state

    still = jnp.zeros((ns, WIDE), F32)
    for cols in chunks:
        main_fin[:, cols] = lax.fori_loop(
            BLOCK // STEP, tok // STEP, lambda i, state: advance(i, state, cols), still
        )

    collect(1, 0, BLOCK)
    forward(0)

    def s_copy(o, src, to):
        return ctx_copy(s_out.at[o], s_in.at[src], s_send.at[o], s_recv.at[src], to)

    share = n_own // len(chunks)
    for q, cols in reversed(list(enumerate(chunks))):
        early = still
        for i in range(BLOCK // STEP):
            early = advance(i, early, cols)
        early_fin[:, cols] = early
        early_gone[:, cols] = jnp.exp2(rate_s[:, cols] * sums_a[0:1, cols])
        final = main_fin[:, cols] + jnp.exp2(rate_s[:, cols] * sums_a[1:2, cols]) * early
        flat = jnp.concatenate([final[:, k * LANES : (k + 1) * LANES] for k in range(WIDE // LANES)], axis=0)
        s_out[q * share : (q + 1) * share] = flat.astype(s_out.dtype).reshape(share, pieces, LANES)

        def send(i):
            o = q * share + i
            to = own_lo + o

            @pl.when(jnp.logical_and(to != me, me < n_ctx - 1))
            def _():
                s_copy(o, me, to).start()

        each(share, send)

    spread_readout()

    scale = LOG2E / math.sqrt(HEAD_WIDTH)
    heads = query.shape[1] // HEAD_WIDTH
    high = group * tok
    bands = decay_a.shape[0] // high
    side = lax.rem(me, 2)
    key_end = jnp.minimum(prompt_end, first)
    diagonal_iota = lax.broadcasted_iota(jnp.int32, (tok, tok), 1)
    allowed = jnp.logical_and(
        diagonal_iota <= lax.broadcasted_iota(jnp.int32, (tok, tok), 0), diagonal_iota + first < prompt_end
    )

    def inner(g):
        return slice(g * tok, (g + 1) * tok)

    def scores_at(p, g):
        base = pl.multiple_of(lax.rem(p, bands) * high + g * tok, tok)
        return pl.ds(base, tok), block_rows(p // bands, 2 * tok)

    def dot_keys(q, keys):
        return lax.dot_general(q, keys, (((1,), (1,)), ((), ())), preferred_element_type=F32)

    def known(p, parity):
        at = lax.broadcasted_iota(jnp.int32, (2 * tok, HEAD_WIDTH), 0)
        return at + jnp.where(at >= tok, tok, 0) + (parity + 4 * p) * tok < key_end

    def both_blocks(p, parity, what):
        one = parity + 4 * p
        two = jnp.minimum(one + 2, me)
        return jnp.concatenate([kv_all[one, what], kv_all[two, what]], axis=0).astype(F32)

    def score(head0, parity, pairs, highest):
        @pl.loop(0, pairs)
        def _(p):
            stand_in = jnp.broadcast_to(kv_all[parity, 0, 0:1, :].astype(F32), (2 * tok, HEAD_WIDTH))
            keys = jnp.where(known(p, parity), both_blocks(p, parity, 0), stand_in).astype(BF16)
            for g in range(group):
                s = dot_keys(query[:, span(head0, g)], keys)
                rows, lanes = scores_at(p, g)
                decay_a[rows, lanes] = s
                highest[inner(g), :] = jnp.maximum(highest[inner(g), :], jnp.maximum(s[:, :tok], s[:, tok:]))

    def gather(parity, pairs):
        @pl.loop(0, pairs)
        def _(p):
            kept = known(p, parity)
            values = jnp.concatenate(
                [jnp.where(kept, both_blocks(p, parity, 1), 0.0), jnp.where(kept, 1.0, 0.0)], axis=1
            ).astype(BF16)
            for g in range(group):
                rows, lanes = scores_at(p, g)
                highest = jnp.concatenate([top[inner(g), :]] * 2, axis=1)
                w = jnp.exp2((decay_a[rows, lanes] - highest) * scale).astype(BF16)
                acc[inner(g), :] += jnp.dot(w, values, preferred_element_type=F32)

    def span(head0, g):
        return slice((head0 + g) * HEAD_WIDTH, (head0 + g + 1) * HEAD_WIDTH)

    def row_max(ref, g):
        return jnp.broadcast_to(jnp.max(ref[inner(g), :], axis=1, keepdims=True), (tok, tok))

    near_pairs = (me // 2 + 1) // 2
    far_pairs = ((me + 1) // 2 + 1) // 2

    def attend_near(head0):
        own_keys = kv_all[me, 0]
        for g in range(group):
            s = jnp.where(allowed, dot_keys(query[:, span(head0, g)], own_keys), LOW)
            own_scores[inner(g), :] = s
            top[inner(g), :] = s
        score(head0, side, near_pairs, top)
        own_values = jnp.concatenate([kv_all[me, 1], jnp.ones((tok, HEAD_WIDTH), BF16)], axis=1)
        for g in range(group):
            highest = row_max(top, g)
            top[inner(g), :] = highest
            w = jnp.exp2((own_scores[inner(g), :] - highest) * scale).astype(BF16)
            acc[inner(g), :] = jnp.dot(w, own_values, preferred_element_type=F32)
        gather(side, near_pairs)

    def attend_far(head0):
        own_scores[...] = top[...]
        score(head0, 1 - side, far_pairs, own_scores)
        for g in range(group):
            highest = row_max(own_scores, g)
            shrunk = jnp.exp2((top[inner(g), :] - highest) * scale)
            acc[inner(g), :] = acc[inner(g), :] * jnp.concatenate([shrunk] * 2, axis=1)
            top[inner(g), :] = highest
        gather(1 - side, far_pairs)
        for g in range(group):
            attn_out[:, span(head0, g)] = (acc[inner(g), :HEAD_WIDTH] / acc[inner(g), HEAD_WIDTH:]).astype(BF16)

    for cols in chunks:
        def shrink(i, gone):
            t0 = pl.multiple_of(i * STEP, STEP)
            for k in range(STEP):
                rows = block_rows(t0 + k, ns)
                gone = gone * decay_a[rows, cols]
                gone_out[rows, cols] = gone.astype(BF16)
            return gone

        whole = jnp.ones((ns, WIDE), F32)
        lax.fori_loop(0, BLOCK // STEP, shrink, whole)
        lax.fori_loop(BLOCK // STEP, tok // STEP, shrink, whole)

    forward(1)

    each(steps - 2, lambda d: forward(d + 2))

    @pl.loop(0, blocks)
    def _(b):
        rows = block_rows(b, BLOCK)
        left = lhs[rows, :]
        for q in range(chans // TILE):
            cols = slice(q * TILE, (q + 1) * TILE)
            gain = jnp.concatenate(
                [skip[g : g + 1, :] for g in range(q * TILE // LANES, (q + 1) * TILE // LANES)], axis=1
            )
            base_y[rows, cols] = gain * conv_out[rows, cols].astype(F32) + jnp.dot(
                left, state_a[block_rows(b, BLOCK * ns), cols], preferred_element_type=F32
            )

    def p_copy(k, o, to):
        return ctx_copy(p_out.at[k], p_in.at[o], p_send.at[k], p_recv.at[o], to)

    @pl.when(is_owner)
    def _():
        o = me - own_lo
        s_in[me] = s_out[o]
        my_rate = rate_flat[pl.ds(o * pieces, pieces), :]

        def send(k):
            @pl.when(k != me)
            def _():
                p_copy(k, o, k).start()

        def weigh(j):
            @pl.when(j != me)
            def _():
                e_copy(j, me, 0).wait_recv()

            if pieces >= ns:
                count = pieces // ns
                gone = jnp.concatenate(
                    [
                        jnp.broadcast_to(e_all[j, pl.ds(o * count + i, 1), :], (ns, LANES))
                        for i in range(count)
                    ],
                    axis=0,
                )
            else:
                gone = jnp.broadcast_to(e_all[j, pl.ds(o * pieces // ns, 1), :], (pieces, LANES))
            block_gone[j] = jnp.exp2(my_rate * gone)

        each(n_ctx - 1, weigh)

        def fold(j, running):
            @pl.when(j != me)
            def _():
                s_copy(0, j, me).wait_recv()

            running = block_gone[j] * running + s_in[j].astype(F32)
            p_out[j + 1] = running.astype(p_out.dtype)
            send(j + 1)
            return running

        running = jnp.zeros((pieces, LANES), F32)
        if n_ctx <= 8:
            for j in range(n_ctx - 1):
                running = fold(j, running)
        else:
            running = lax.fori_loop(0, n_ctx - 1, fold, running)

        p_in[o] = p_out[me]

    @pl.loop(0, ch)
    def _(g):
        lanes = block_rows(g, LANES)
        gate_out[:, lanes] = silu(gate[:, lanes].astype(F32))

    attend_near(0)

    def arrive(d):
        src = twin - 2 * (d + 1)

        @pl.when(src >= 0)
        def _():
            kv_copy(src, twin, kv_send.at[src]).wait_recv()

    each(steps, arrive)

    @pl.when(lax.rem(me, 2) == 1)
    def _():
        kv_copy(me - 1, twin, kv_send.at[0]).wait_recv()

    attend_far(0)
    for head0 in range(group, heads, group):
        attend_near(head0)
        attend_far(head0)

    @pl.when(me < n_ctx - 1)
    def _():
        halo.wait_send()
        owners(lambda o, to: e_copy(me, to, o).wait_send())
        owners(lambda o, to: s_copy(o, me, to).wait_send())

    for late in range(2):
        peers(lambda to: part_copy(late, mt, to).wait_send())
    kv_line(lambda to: kv_copy(me, to, kv_send.at[to]).wait_send())

    def end_forward(d):
        src = me - 2 * (d + 1)

        @pl.when(src >= 0)
        def _():
            kv_copy(src, twin, kv_forward.at[src]).wait_send()

    each(steps, end_forward)

    @pl.when(is_owner)
    def _():
        def sent(k):
            @pl.when(k + 1 != me)
            def _():
                p_copy(k + 1, 0, k + 1).wait_send()

        each(n_ctx - 1, sent)

    @pl.when(me > 0)
    def _():
        owners(lambda o, to: p_copy(0, o, me).wait_recv())

    @pl.when(me == 0)
    def _():
        p_in[...] = jnp.zeros_like(p_in)

    entering = p_in[...].reshape(ns * ch, LANES).astype(F32)
    for g in range(ch):
        lanes = slice(g * LANES, (g + 1) * LANES)
        now = entering[g * ns : (g + 1) * ns, :]
        inc_out[0, :, lanes] = now.astype(BF16)
        inc_out[1, :, lanes] = (early_fin[:, lanes] + early_gone[:, lanes] * now).astype(BF16)


def last_kernel(
    gone, base_y, gate, inc, lhs, attn, mamba_out_hbm, attn_out_hbm, out, attn_sem, out_sem
):
    tok, chans = base_y.shape
    ns = inc.shape[1]
    attn_store = pltpu.make_async_copy(attn, attn_out_hbm, attn_sem)
    attn_store.start()
    stores = []
    for q in range(chans // TILE):
        cols = slice(q * TILE, (q + 1) * TILE)
        for b in range(tok // BLOCK):
            rows = slice(b * BLOCK, (b + 1) * BLOCK)
            held = gone[b * BLOCK * ns : (b + 1) * BLOCK * ns, cols].reshape(BLOCK, ns, TILE)
            held = (held * inc[min(b, 1), :, cols][None]).reshape(BLOCK * ns, TILE)
            y = base_y[rows, cols] + jnp.dot(lhs[rows, :], held, preferred_element_type=F32)
            out[rows, cols] = (y * gate[rows, cols]).astype(BF16)
        stores.append(pltpu.make_async_copy(out.at[:, cols], mamba_out_hbm.at[:, cols], out_sem.at[q]))
        stores[-1].start()
    attn_store.wait()
    for store in stores:
        store.wait()


def shards(
    n_ctx, n_ten,
    length, mamba_in, gate_in, step_raw, conv_weight, conv_bias, step_bias, decay_rates, skip_gain,
    state_proj, query_input_rows, key_input_rows, value_input_rows,
):
    tok, chans = mamba_in.shape
    ch = chans // LANES
    ns = decay_rates.shape[0]
    heads = query_input_rows.shape[1] // HEAD_WIDTH
    group = heads
    while group > 1 and n_ctx * group * tok * LANES > tok * ns * chans:
        group //= 2
    own_lo, n_own = n_ctx // 4, n_ctx // 2
    pieces = ns * ch // n_own
    link = BF16 if pieces % 16 == 0 else F32
    dma = pltpu.SemaphoreType.DMA
    hbm = pl.BlockSpec(memory_space=pl.ANY)
    vmem = pl.BlockSpec(memory_space=pltpu.VMEM)
    ordered = (
        length, mamba_in, step_raw, conv_weight, step_bias.reshape(ch, LANES), decay_rates,
        conv_bias.reshape(ch, LANES), state_proj.T, gate_in, key_input_rows, value_input_rows,
        skip_gain.reshape(ch, LANES), query_input_rows,
    )
    held = [pltpu.SMEM((1,), jnp.int32)]
    held += [pltpu.VMEM(a.shape, a.dtype) for i, a in enumerate(ordered) if i not in (0, 9, 10)]
    channels = pltpu.VMEM((ns, chans), F32)
    halo = ((KW - 1) * ch, LANES)
    parts = pl.pallas_call(
        functools.partial(main_kernel, n_ctx, n_ten, group, own_lo, n_own),
        out_shape=(
            pltpu.VMEM((tok * ns, chans), BF16),
            pltpu.VMEM((tok, chans), F32),
            pltpu.VMEM((tok, chans), F32),
            pltpu.VMEM((2, ns, chans), BF16),
            pltpu.VMEM((tok, BLOCK * ns), BF16),
            pltpu.VMEM(query_input_rows.shape, BF16),
        ),
        in_specs=[hbm] * 13,
        out_specs=(vmem,) * 6,
        scratch_shapes=held + [
            pltpu.VMEM((ch, tok + 8, LANES), F32),
            pltpu.VMEM((tok, chans), BF16),
            pltpu.VMEM((tok, chans), F32),
            pltpu.VMEM((tok, chans), F32),
            channels,
            pltpu.VMEM((ns * ch, LANES), F32),
            pltpu.VMEM((2, chans), F32),
            pltpu.VMEM((tok * ns, LANES), F32),
            pltpu.VMEM((tok * ns, chans), F32),
            pltpu.VMEM((tok * ns, chans), BF16),
            channels,
            channels,
            channels,
            pltpu.VMEM((2, ns, tok), F32),
            pltpu.VMEM((n_ctx, pieces, LANES), F32),
            pltpu.VMEM(halo, F32), pltpu.VMEM(halo, BF16), pltpu.VMEM(halo, BF16),
            pltpu.VMEM((2, n_ten, 2 * ns, tok), F32),
            pltpu.VMEM((n_ctx, ch, LANES), F32),
            pltpu.VMEM((n_own, pieces, LANES), link),
            pltpu.VMEM((n_ctx, pieces, LANES), link),
            pltpu.VMEM((n_ctx, pieces, LANES), link),
            pltpu.VMEM((n_own, pieces, LANES), link),
            pltpu.VMEM((n_ctx, 2, tok, HEAD_WIDTH), BF16),
            pltpu.VMEM((group * tok, tok), F32),
            pltpu.VMEM((group * tok, tok), F32),
            pltpu.VMEM((group * tok, 2 * HEAD_WIDTH), F32),
            dma, dma, dma((2, n_ten)), dma((2, n_ten)),
            dma((n_own,)), dma((n_ctx,)), dma((n_ctx,)), dma((n_own,)),
            dma((n_own,)), dma((n_ctx,)), dma((n_ctx,)), dma((n_ctx,)), dma((n_ctx,)),
            dma((len(ordered),)),
        ],
        compiler_params=pltpu.CompilerParams(
            collective_id=0, has_side_effects=True, vmem_limit_bytes=48 << 20
        ),
    )(*ordered)
    return pl.pallas_call(
        last_kernel,
        out_shape=(
            jax.ShapeDtypeStruct(mamba_in.shape, BF16),
            jax.ShapeDtypeStruct(query_input_rows.shape, BF16),
        ),
        in_specs=[vmem] * 6,
        out_specs=(hbm, hbm),
        scratch_shapes=[pltpu.VMEM((tok, chans), BF16), dma, dma((chans // TILE,))],
        compiler_params=pltpu.CompilerParams(vmem_limit_bytes=16 << 20),
    )(*parts)


def solution(mesh):
    both = P("context", "tensor")
    in_specs = (
        P(), both, both, both, P(None, "tensor"), P("tensor"), P("tensor"), P(None, "tensor"),
        P("tensor"), P("tensor", None), both, both, both,
    )
    body = functools.partial(shards, mesh.shape["context"], mesh.shape["tensor"])
    return jax.shard_map(body, mesh=mesh, in_specs=in_specs, out_specs=(both, both), check_vma=False)
```

```python
import functools
import math

import jax
import jax.numpy as jnp
from jax import lax
from jax.experimental import pallas as pl
from jax.experimental.pallas import tpu as pltpu
from jax.sharding import PartitionSpec as P

KW = 4
HEAD_WIDTH = 128
LANES = 128
BLOCK = 16
WIDE = 512
STEP = 8
TILE = 256
LOG2E = 1.4426950408889634
LOW = -1e30
MESH = pl.DeviceIdType.MESH
F32 = jnp.float32
BF16 = jnp.bfloat16


def each(count, body):
    if count <= 8:
        for i in range(count):
            body(i)
    else:
        @pl.loop(0, count)
        def _(i):
            body(i)


def silu(v):
    return v / (1.0 + jnp.exp(-v))


def block_rows(b, size):
    return pl.ds(pl.multiple_of(b * size, size), size)


def main_kernel(
    n_ctx, n_ten, group, own_lo, n_own,
    length_hbm, mamba_hbm, step_hbm, conv_w_hbm, step_b_hbm, rates_hbm, conv_b_hbm, proj_hbm, gate_hbm,
    keys_hbm, values_hbm, skip_hbm, query_hbm,
    gone_out, base_y, gate_out, inc_out, lhs, attn_out,
    length, mamba, step_raw, conv_w, step_b, rates, conv_b, proj, gate, skip, query,
    x_a, conv_out, step_a, driven, rate_s, rate_flat, sums_a, spread, decay_a, state_a, main_fin, early_fin, early_gone, part_sum, block_gone,
    halo_f, halo_out, halo_in, part_all, e_all, s_out, s_in, p_out, p_in, kv_all, top, own_scores, acc,
    halo_send, halo_recv, part_send, part_recv, s_send, s_recv, p_send, p_recv, e_send, e_recv,
    kv_send, kv_recv, kv_forward, load_sem,
):
    tok, chans = mamba.shape
    ch = chans // LANES
    ns = rates.shape[0]
    blocks = tok // BLOCK
    pieces = s_out.shape[1]
    me = lax.axis_index("context")
    mt = lax.axis_index("tensor")

    def ctx_copy(src, dst, send, recv, to):
        return pltpu.make_async_remote_copy(
            src_ref=src, dst_ref=dst, send_sem=send, recv_sem=recv,
            device_id={"context": to}, device_id_type=MESH,
        )

    sources = (
        mamba_hbm, step_hbm, length_hbm, conv_w_hbm, step_b_hbm, rates_hbm, conv_b_hbm, proj_hbm, gate_hbm,
        keys_hbm, values_hbm, skip_hbm, query_hbm,
    )
    targets = (
        mamba, step_raw, length, conv_w, step_b, rates, conv_b, proj, gate,
        kv_all.at[me, 0], kv_all.at[me, 1], skip, query,
    )
    loads = [
        pltpu.make_async_copy(src, dst, load_sem.at[i])
        for i, (src, dst) in enumerate(zip(sources, targets))
    ]
    for load in loads[:2]:
        load.start()

    barrier = pltpu.get_barrier_semaphore()
    for d in range(1, n_ten):
        pl.semaphore_signal(
            barrier, inc=1, device_id={"tensor": lax.rem(mt + d, n_ten)}, device_id_type=MESH
        )

    def owns(k):
        return jnp.logical_and(k >= own_lo, k < own_lo + n_own)

    is_owner = owns(me)

    def meets(k):
        near = jnp.logical_or(lax.rem(k - me + n_ctx, 2) == 0, jnp.abs(k - me) == 1)
        return jnp.logical_or(jnp.logical_or(owns(k), is_owner), near)

    def greet(to):
        @pl.when(meets(to))
        def _():
            pl.semaphore_signal(barrier, inc=1, device_id={"context": to}, device_id_type=MESH)

    each(n_ctx - 1, lambda d: greet(lax.rem(me + d + 1, n_ctx)))

    def count_met(d, total):
        return total + jnp.where(meets(lax.rem(me + d + 1, n_ctx)), 1, 0)

    met = jnp.int32(n_ten - 1)
    if n_ctx <= 8:
        for d in range(n_ctx - 1):
            met = count_met(d, met)
    else:
        met = lax.fori_loop(0, n_ctx - 1, count_met, met)

    for load in loads[2:]:
        load.start()

    first = me * tok
    for load in loads[:7]:
        load.wait()
    prompt_end = length[0]
    valid = (first + lax.broadcasted_iota(jnp.int32, (tok, LANES), 0)) < prompt_end
    conv_out[0:BLOCK, :] = jnp.zeros((BLOCK, chans), BF16)

    def convolve(g, lanes, start, count):
        total = jnp.broadcast_to(conv_b[pl.ds(g, 1), :], (count, LANES))
        for j in range(KW):
            at = 8 + start - (KW - 1) + j
            total = total + conv_w[j : j + 1, lanes] * x_a[g, at : at + count, :]
        mixed = silu(total).astype(BF16)
        conv_out[start : start + count, lanes] = mixed
        driven[start : start + count, lanes] = step_a[start : start + count, lanes] * mixed.astype(F32)

    @pl.loop(0, ch)
    def _(g):
        lanes = block_rows(g, LANES)
        x = mamba[:, lanes].astype(F32)
        x_a[g, 8 : 8 + tok, :] = x
        for j in range(KW - 1):
            at = tok - (KW - 1) + j
            halo_f[pl.ds(j * ch + g, 1), :] = x[at : at + 1, :]
        raw = step_raw[:, lanes].astype(F32) + step_b[pl.ds(g, 1), :]
        size = jnp.maximum(raw, 0.0) + jnp.log(1.0 + jnp.exp(-jnp.abs(raw)))
        size = jnp.where(valid, size, 0.0)
        step_a[:, lanes] = size
        early = jnp.sum(size[:BLOCK], axis=0, keepdims=True)
        late = jnp.sum(size[BLOCK:], axis=0, keepdims=True)
        sums_a[0:1, lanes] = early
        sums_a[1:2, lanes] = late
        e_all[me, pl.ds(g, 1), :] = early + late
        scaled = rates[:, lanes] * (-LOG2E)
        rate_s[:, lanes] = scaled
        rate_flat[block_rows(g, ns), :] = scaled
        convolve(g, lanes, BLOCK, tok - BLOCK)

    halo_out[...] = halo_f[...].astype(BF16)
    loads[7].wait()

    def partial_projection(count):
        return lax.dot_general(
            proj[...], conv_out[0:count, :], (((1,), (1,)), ((), ())), preferred_element_type=F32
        )

    part_all[0, mt] = partial_projection(tok)

    for load in loads[8:]:
        load.wait()

    pl.semaphore_wait(barrier, met)

    halo = ctx_copy(halo_out, halo_in, halo_send, halo_recv, lax.rem(me + 1, n_ctx))

    @pl.when(me < n_ctx - 1)
    def _():
        halo.start()

    def part_copy(late, src, to):
        return pltpu.make_async_remote_copy(
            src_ref=part_all.at[late, src], dst_ref=part_all.at[late, src],
            send_sem=part_send.at[late, to], recv_sem=part_recv.at[late, src],
            device_id={"tensor": to}, device_id_type=MESH,
        )

    def peers(body):
        for d in range(1, n_ten):
            body(lax.rem(mt + d, n_ten))

    peers(lambda to: part_copy(0, mt, to).start())

    def owners(body):
        def visit(o):
            to = own_lo + o

            @pl.when(to != me)
            def _():
                body(o, to)

        each(n_own, visit)

    def e_copy(src, to, slot):
        return ctx_copy(e_all.at[src], e_all.at[src], e_send.at[slot], e_recv.at[src], to)

    @pl.when(me < n_ctx - 1)
    def _():
        owners(lambda o, to: e_copy(me, to, o).start())

    twin = me + 1 - 2 * lax.rem(me, 2)
    steps = n_ctx // 2 - 1

    def kv_copy(src, to, send):
        return ctx_copy(kv_all.at[src], kv_all.at[src], send, kv_recv.at[src], to)

    def kv_line(body):
        def visit(d):
            to = me + 2 * (d + 1)

            @pl.when(to < n_ctx)
            def _():
                body(to)

        each(n_ctx // 2 - 1, visit)

        @pl.when(lax.rem(me, 2) == 0)
        def _():
            body(me + 1)

    kv_line(lambda to: kv_copy(me, to, kv_send.at[to]).start())

    def forward(d):
        src = me - 2 * (d + 1)

        @pl.when(src >= 0)
        def _():
            kv_copy(src, twin, kv_forward.at[src]).wait_recv()
            kv_copy(src, twin, kv_forward.at[src]).start()

    chunks = [slice(q * WIDE, (q + 1) * WIDE) for q in range(chans // WIDE)]

    def decays(i):
        t0 = pl.multiple_of(i * STEP, STEP)
        for q in range(chans // TILE):
            cols = slice(q * TILE, (q + 1) * TILE)
            rate = rate_s[:, cols]
            for k in range(STEP):
                size = jnp.broadcast_to(step_a[pl.ds(t0 + k, 1), cols], (ns, TILE))
                decay_a[block_rows(t0 + k, ns), cols] = jnp.exp2(rate * size)

    pl.loop(0, tok // STEP * 7 // 8)(decays)

    @pl.when(me > 0)
    def _():
        halo.wait_recv()
        halo_f[...] = halo_in[...].astype(F32)

    @pl.when(me == 0)
    def _():
        halo_f[...] = jnp.zeros_like(halo_f)

    @pl.loop(0, ch // 4)
    def _(i):
        for g in [i * 4 + k for k in range(4)]:
            for j in range(KW - 1):
                at = 8 - (KW - 1) + j
                x_a[g, at : at + 1, :] = halo_f[pl.ds(j * ch + g, 1), :]
        for g in [i * 4 + k for k in range(4)]:
            convolve(g, block_rows(g, LANES), 0, BLOCK)

    part_all[1, mt] = jnp.concatenate(
        [partial_projection(BLOCK), jnp.zeros((2 * ns, tok - BLOCK), F32)], axis=1
    )
    peers(lambda to: part_copy(1, mt, to).start())
    pl.loop(tok // STEP * 7 // 8, tok // STEP)(decays)

    def collect(late, start, stop):
        peers(lambda src: part_copy(late, src, mt).wait_recv())
        projected = part_all[late, 0]
        for d in range(1, n_ten):
            projected = projected + part_all[late, d]
        for t in range(start, stop):
            spread[t * ns : (t + 1) * ns, :] = jnp.broadcast_to(projected[:ns, t : t + 1], (ns, LANES))
        part_sum[late] = projected[ns:]

    def spread_readout():
        early = lax.broadcasted_iota(jnp.int32, (ns, tok), 1) < BLOCK
        readout = jnp.where(early, part_sum[1], part_sum[0])
        source = lax.broadcasted_iota(jnp.int32, (ns, BLOCK * ns), 0)
        entry = lax.rem(lax.broadcasted_iota(jnp.int32, (ns, BLOCK * ns), 1), ns)
        pick = jnp.where(source == entry, 1.0, 0.0).astype(BF16)
        wide = jnp.dot(readout.T.astype(BF16), pick, preferred_element_type=F32)
        token = lax.rem(lax.broadcasted_iota(jnp.int32, wide.shape, 0), BLOCK)
        owner = lax.broadcasted_iota(jnp.int32, wide.shape, 1) // ns
        lhs[...] = jnp.where(token == owner, wide, 0.0).astype(BF16)

    collect(0, BLOCK, tok)

    def advance(i, state, cols):
        t0 = pl.multiple_of(i * STEP, STEP)
        for k in range(STEP):
            rows = block_rows(t0 + k, ns)
            inject = jnp.concatenate([spread[rows, :]] * (WIDE // LANES), axis=1)
            drive = inject * jnp.broadcast_to(driven[pl.ds(t0 + k, 1), cols], (ns, WIDE))
            state = decay_a[rows, cols] * state + drive
            state_a[rows, cols] = state.astype(BF16)
        return state

    still = jnp.zeros((ns, WIDE), F32)
    for cols in chunks:
        main_fin[:, cols] = lax.fori_loop(
            BLOCK // STEP, tok // STEP, lambda i, state: advance(i, state, cols), still
        )

    collect(1, 0, BLOCK)
    forward(0)

    def s_copy(o, src, to):
        return ctx_copy(s_out.at[o], s_in.at[src], s_send.at[o], s_recv.at[src], to)

    share = n_own // len(chunks)
    for q, cols in reversed(list(enumerate(chunks))):
        early = still
        for i in range(BLOCK // STEP):
            early = advance(i, early, cols)
        early_fin[:, cols] = early
        early_gone[:, cols] = jnp.exp2(rate_s[:, cols] * sums_a[0:1, cols])
        final = main_fin[:, cols] + jnp.exp2(rate_s[:, cols] * sums_a[1:2, cols]) * early
        flat = jnp.concatenate([final[:, k * LANES : (k + 1) * LANES] for k in range(WIDE // LANES)], axis=0)
        s_out[q * share : (q + 1) * share] = flat.astype(s_out.dtype).reshape(share, pieces, LANES)

        def send(i):
            o = q * share + i
            to = own_lo + o

            @pl.when(jnp.logical_and(to != me, me < n_ctx - 1))
            def _():
                s_copy(o, me, to).start()

        each(share, send)

    spread_readout()

    scale = LOG2E / math.sqrt(HEAD_WIDTH)
    heads = query.shape[1] // HEAD_WIDTH
    high = group * tok
    bands = decay_a.shape[0] // high
    side = lax.rem(me, 2)
    key_end = jnp.minimum(prompt_end, first)
    diagonal_iota = lax.broadcasted_iota(jnp.int32, (tok, tok), 1)
    allowed = jnp.logical_and(
        diagonal_iota <= lax.broadcasted_iota(jnp.int32, (tok, tok), 0), diagonal_iota + first < prompt_end
    )

    def inner(g):
        return slice(g * tok, (g + 1) * tok)

    def scores_at(p, g):
        base = pl.multiple_of(lax.rem(p, bands) * high + g * tok, tok)
        return pl.ds(base, tok), block_rows(p // bands, 2 * tok)

    def dot_keys(q, keys):
        return lax.dot_general(q, keys, (((1,), (1,)), ((), ())), preferred_element_type=F32)

    def known(p, parity):
        at = lax.broadcasted_iota(jnp.int32, (2 * tok, HEAD_WIDTH), 0)
        return at + jnp.where(at >= tok, tok, 0) + (parity + 4 * p) * tok < key_end

    def both_blocks(p, parity, what):
        one = parity + 4 * p
        two = jnp.minimum(one + 2, me)
        return jnp.concatenate([kv_all[one, what], kv_all[two, what]], axis=0).astype(F32)

    def score(head0, parity, pairs, highest):
        @pl.loop(0, pairs)
        def _(p):
            stand_in = jnp.broadcast_to(kv_all[parity, 0].astype(F32)[0:1], (2 * tok, HEAD_WIDTH))
            keys = jnp.where(known(p, parity), both_blocks(p, parity, 0), stand_in).astype(BF16)
            for g in range(group):
                s = dot_keys(query[:, span(head0, g)], keys)
                rows, lanes = scores_at(p, g)
                decay_a[rows, lanes] = s
                highest[inner(g), :] = jnp.maximum(highest[inner(g), :], jnp.maximum(s[:, :tok], s[:, tok:]))

    def gather(parity, pairs):
        @pl.loop(0, pairs)
        def _(p):
            kept = known(p, parity)
            values = jnp.concatenate(
                [jnp.where(kept, both_blocks(p, parity, 1), 0.0), jnp.where(kept, 1.0, 0.0)], axis=1
            ).astype(BF16)
            for g in range(group):
                rows, lanes = scores_at(p, g)
                highest = jnp.concatenate([top[inner(g), :]] * 2, axis=1)
                w = jnp.exp2((decay_a[rows, lanes] - highest) * scale).astype(BF16)
                acc[inner(g), :] += jnp.dot(w, values, preferred_element_type=F32)

    def span(head0, g):
        return slice((head0 + g) * HEAD_WIDTH, (head0 + g + 1) * HEAD_WIDTH)

    def row_max(ref, g):
        return jnp.broadcast_to(jnp.max(ref[inner(g), :], axis=1, keepdims=True), (tok, tok))

    near_pairs = (me // 2 + 1) // 2
    far_pairs = ((me + 1) // 2 + 1) // 2

    def attend_near(head0):
        own_keys = kv_all[me, 0]
        for g in range(group):
            s = jnp.where(allowed, dot_keys(query[:, span(head0, g)], own_keys), LOW)
            own_scores[inner(g), :] = s
            top[inner(g), :] = s
        score(head0, side, near_pairs, top)
        own_values = jnp.concatenate([kv_all[me, 1], jnp.ones((tok, HEAD_WIDTH), BF16)], axis=1)
        for g in range(group):
            highest = row_max(top, g)
            top[inner(g), :] = highest
            w = jnp.exp2((own_scores[inner(g), :] - highest) * scale).astype(BF16)
            acc[inner(g), :] = jnp.dot(w, own_values, preferred_element_type=F32)
        gather(side, near_pairs)

    def attend_far(head0):
        own_scores[...] = top[...]
        score(head0, 1 - side, far_pairs, own_scores)
        for g in range(group):
            highest = row_max(own_scores, g)
            shrunk = jnp.exp2((top[inner(g), :] - highest) * scale)
            acc[inner(g), :] = acc[inner(g), :] * jnp.concatenate([shrunk] * 2, axis=1)
            top[inner(g), :] = highest
        gather(1 - side, far_pairs)
        for g in range(group):
            attn_out[:, span(head0, g)] = (acc[inner(g), :HEAD_WIDTH] / acc[inner(g), HEAD_WIDTH:]).astype(BF16)

    for cols in chunks:
        def shrink(i, gone):
            t0 = pl.multiple_of(i * STEP, STEP)
            for k in range(STEP):
                rows = block_rows(t0 + k, ns)
                gone = gone * decay_a[rows, cols]
                gone_out[rows, cols] = gone.astype(BF16)
            return gone

        whole = jnp.ones((ns, WIDE), F32)
        lax.fori_loop(0, BLOCK // STEP, shrink, whole)
        lax.fori_loop(BLOCK // STEP, tok // STEP, shrink, whole)

    forward(1)

    each(steps - 2, lambda d: forward(d + 2))

    @pl.loop(0, blocks)
    def _(b):
        rows = block_rows(b, BLOCK)
        left = lhs[rows, :]
        for q in range(chans // TILE):
            cols = slice(q * TILE, (q + 1) * TILE)
            gain = jnp.concatenate(
                [skip[g : g + 1, :] for g in range(q * TILE // LANES, (q + 1) * TILE // LANES)], axis=1
            )
            base_y[rows, cols] = gain * conv_out[rows, cols].astype(F32) + jnp.dot(
                left, state_a[block_rows(b, BLOCK * ns), cols], preferred_element_type=F32
            )

    def p_copy(k, o, to):
        return ctx_copy(p_out.at[k], p_in.at[o], p_send.at[k], p_recv.at[o], to)

    @pl.when(is_owner)
    def _():
        o = me - own_lo
        s_in[me] = s_out[o]
        my_rate = rate_flat[pl.ds(o * pieces, pieces), :]

        def send(k):
            @pl.when(k != me)
            def _():
                p_copy(k, o, k).start()

        def weigh(j):
            @pl.when(j != me)
            def _():
                e_copy(j, me, 0).wait_recv()

            if pieces >= ns:
                count = pieces // ns
                gone = jnp.concatenate(
                    [
                        jnp.broadcast_to(e_all[j, pl.ds(o * count + i, 1), :], (ns, LANES))
                        for i in range(count)
                    ],
                    axis=0,
                )
            else:
                gone = jnp.broadcast_to(e_all[j, pl.ds(o * pieces // ns, 1), :], (pieces, LANES))
            block_gone[j] = jnp.exp2(my_rate * gone)

        each(n_ctx - 1, weigh)

        def fold(j, running):
            @pl.when(j != me)
            def _():
                s_copy(0, j, me).wait_recv()

            running = block_gone[j] * running + s_in[j].astype(F32)
            p_out[j + 1] = running.astype(p_out.dtype)
            send(j + 1)
            return running

        running = jnp.zeros((pieces, LANES), F32)
        if n_ctx <= 8:
            for j in range(n_ctx - 1):
                running = fold(j, running)
        else:
            running = lax.fori_loop(0, n_ctx - 1, fold, running)

        p_in[o] = p_out[me]

    @pl.loop(0, ch)
    def _(g):
        lanes = block_rows(g, LANES)
        gate_out[:, lanes] = silu(gate[:, lanes].astype(F32))

    attend_near(0)

    def arrive(d):
        src = twin - 2 * (d + 1)

        @pl.when(src >= 0)
        def _():
            kv_copy(src, twin, kv_send.at[src]).wait_recv()

    each(steps, arrive)

    @pl.when(lax.rem(me, 2) == 1)
    def _():
        kv_copy(me - 1, twin, kv_send.at[0]).wait_recv()

    attend_far(0)
    for head0 in range(group, heads, group):
        attend_near(head0)
        attend_far(head0)

    @pl.when(me < n_ctx - 1)
    def _():
        halo.wait_send()
        owners(lambda o, to: e_copy(me, to, o).wait_send())
        owners(lambda o, to: s_copy(o, me, to).wait_send())

    for late in range(2):
        peers(lambda to: part_copy(late, mt, to).wait_send())
    kv_line(lambda to: kv_copy(me, to, kv_send.at[to]).wait_send())

    def end_forward(d):
        src = me - 2 * (d + 1)

        @pl.when(src >= 0)
        def _():
            kv_copy(src, twin, kv_forward.at[src]).wait_send()

    each(steps, end_forward)

    @pl.when(is_owner)
    def _():
        def sent(k):
            @pl.when(k + 1 != me)
            def _():
                p_copy(k + 1, 0, k + 1).wait_send()

        each(n_ctx - 1, sent)

    @pl.when(me > 0)
    def _():
        owners(lambda o, to: p_copy(0, o, me).wait_recv())

    @pl.when(me == 0)
    def _():
        p_in[...] = jnp.zeros_like(p_in)

    entering = p_in[...].reshape(ns * ch, LANES).astype(F32)
    for g in range(ch):
        lanes = slice(g * LANES, (g + 1) * LANES)
        now = entering[g * ns : (g + 1) * ns, :]
        inc_out[0, :, lanes] = now.astype(BF16)
        inc_out[1, :, lanes] = (early_fin[:, lanes] + early_gone[:, lanes] * now).astype(BF16)


def last_kernel(
    gone, base_y, gate, inc, lhs, attn, mamba_out_hbm, attn_out_hbm, out, attn_sem, out_sem
):
    tok, chans = base_y.shape
    ns = inc.shape[1]
    attn_store = pltpu.make_async_copy(attn, attn_out_hbm, attn_sem)
    attn_store.start()
    stores = []
    for q in range(chans // TILE):
        cols = slice(q * TILE, (q + 1) * TILE)
        for b in range(tok // BLOCK):
            rows = slice(b * BLOCK, (b + 1) * BLOCK)
            held = gone[b * BLOCK * ns : (b + 1) * BLOCK * ns, cols].reshape(BLOCK, ns, TILE)
            held = (held * inc[min(b, 1), :, cols][None]).reshape(BLOCK * ns, TILE)
            y = base_y[rows, cols] + jnp.dot(lhs[rows, :], held, preferred_element_type=F32)
            out[rows, cols] = (y * gate[rows, cols]).astype(BF16)
        stores.append(pltpu.make_async_copy(out.at[:, cols], mamba_out_hbm.at[:, cols], out_sem.at[q]))
        stores[-1].start()
    attn_store.wait()
    for store in stores:
        store.wait()


def shards(
    n_ctx, n_ten,
    length, mamba_in, gate_in, step_raw, conv_weight, conv_bias, step_bias, decay_rates, skip_gain,
    state_proj, query_input_rows, key_input_rows, value_input_rows,
):
    tok, chans = mamba_in.shape
    ch = chans // LANES
    ns = decay_rates.shape[0]
    heads = query_input_rows.shape[1] // HEAD_WIDTH
    group = heads
    while group > 1 and n_ctx * group * tok * LANES > tok * ns * chans:
        group //= 2
    own_lo, n_own = n_ctx // 4, n_ctx // 2
    pieces = ns * ch // n_own
    link = BF16 if pieces % 16 == 0 else F32
    dma = pltpu.SemaphoreType.DMA
    hbm = pl.BlockSpec(memory_space=pl.ANY)
    vmem = pl.BlockSpec(memory_space=pltpu.VMEM)
    ordered = (
        length, mamba_in, step_raw, conv_weight, step_bias.reshape(ch, LANES), decay_rates,
        conv_bias.reshape(ch, LANES), state_proj.T, gate_in, key_input_rows, value_input_rows,
        skip_gain.reshape(ch, LANES), query_input_rows,
    )
    held = [pltpu.SMEM((1,), jnp.int32)]
    held += [pltpu.VMEM(a.shape, a.dtype) for i, a in enumerate(ordered) if i not in (0, 9, 10)]
    channels = pltpu.VMEM((ns, chans), F32)
    halo = ((KW - 1) * ch, LANES)
    parts = pl.pallas_call(
        functools.partial(main_kernel, n_ctx, n_ten, group, own_lo, n_own),
        out_shape=(
            pltpu.VMEM((tok * ns, chans), BF16),
            pltpu.VMEM((tok, chans), F32),
            pltpu.VMEM((tok, chans), F32),
            pltpu.VMEM((2, ns, chans), BF16),
            pltpu.VMEM((tok, BLOCK * ns), BF16),
            pltpu.VMEM(query_input_rows.shape, BF16),
        ),
        in_specs=[hbm] * 13,
        out_specs=(vmem,) * 6,
        scratch_shapes=held + [
            pltpu.VMEM((ch, tok + 8, LANES), F32),
            pltpu.VMEM((tok, chans), BF16),
            pltpu.VMEM((tok, chans), F32),
            pltpu.VMEM((tok, chans), F32),
            channels,
            pltpu.VMEM((ns * ch, LANES), F32),
            pltpu.VMEM((2, chans), F32),
            pltpu.VMEM((tok * ns, LANES), F32),
            pltpu.VMEM((tok * ns, chans), F32),
            pltpu.VMEM((tok * ns, chans), BF16),
            channels,
            channels,
            channels,
            pltpu.VMEM((2, ns, tok), F32),
            pltpu.VMEM((n_ctx, pieces, LANES), F32),
            pltpu.VMEM(halo, F32), pltpu.VMEM(halo, BF16), pltpu.VMEM(halo, BF16),
            pltpu.VMEM((2, n_ten, 2 * ns, tok), F32),
            pltpu.VMEM((n_ctx, ch, LANES), F32),
            pltpu.VMEM((n_own, pieces, LANES), link),
            pltpu.VMEM((n_ctx, pieces, LANES), link),
            pltpu.VMEM((n_ctx, pieces, LANES), link),
            pltpu.VMEM((n_own, pieces, LANES), link),
            pltpu.VMEM((n_ctx, 2, tok, HEAD_WIDTH), BF16),
            pltpu.VMEM((group * tok, tok), F32),
            pltpu.VMEM((group * tok, tok), F32),
            pltpu.VMEM((group * tok, 2 * HEAD_WIDTH), F32),
            dma, dma, dma((2, n_ten)), dma((2, n_ten)),
            dma((n_own,)), dma((n_ctx,)), dma((n_ctx,)), dma((n_own,)),
            dma((n_own,)), dma((n_ctx,)), dma((n_ctx,)), dma((n_ctx,)), dma((n_ctx,)),
            dma((len(ordered),)),
        ],
        compiler_params=pltpu.CompilerParams(
            collective_id=0, has_side_effects=True, vmem_limit_bytes=48 << 20
        ),
    )(*ordered)
    return pl.pallas_call(
        last_kernel,
        out_shape=(
            jax.ShapeDtypeStruct(mamba_in.shape, BF16),
            jax.ShapeDtypeStruct(query_input_rows.shape, BF16),
        ),
        in_specs=[vmem] * 6,
        out_specs=(hbm, hbm),
        scratch_shapes=[pltpu.VMEM((tok, chans), BF16), dma, dma((chans // TILE,))],
        compiler_params=pltpu.CompilerParams(vmem_limit_bytes=16 << 20),
    )(*parts)


def solution(mesh):
    both = P("context", "tensor")
    in_specs = (
        P(), both, both, both, P(None, "tensor"), P("tensor"), P("tensor"), P(None, "tensor"),
        P("tensor"), P("tensor", None), both, both, both,
    )
    body = functools.partial(shards, mesh.shape["context"], mesh.shape["tensor"])
    return jax.shard_map(body, mesh=mesh, in_specs=in_specs, out_specs=(both, both), check_vma=False)
```
